32 devices in a mesh: gx: 8 (over z, x), gy: 4 (over y, core).
Axes of the slice: x: 2, y: 2, z: 4, core: 2. Of those that a mesh axis runs over, the one named last changes fastest.
Arguments:
- tracer: float32 [128, 64, 256], P('gx', 'gy'), may hold values from -6 to 6
- tensor: float32 [3, 128, 64, 256], P(None, 'gx', 'gy'), may hold values from 0.02 to 0.15
- pressure: float32 [128, 64, 256], P('gx', 'gy'), may hold values from -6 to 6
- observed: float32 [128, 64, 256], P('gx', 'gy'), may hold values from -6 to 6
- depth: int32 [128, 64], P('gx', 'gy'), may hold values from 0 to 256
- cell: int32 [32, 32, 128], P(('gx', 'gy')), may hold values from 0 to 65535
- parent: int32 [32, 32, 128], P(('gx', 'gy')), may hold values from 0 to 4095, as said below
- counts: int32 [32, 32], P(('gx', 'gy')), may hold values from 1 to 128, as said below
- perm: float32 [32, 32, 128], P(('gx', 'gy')), may hold values from 0.05 to 0.5
- filt: float32 [32, 32, 128], P(('gx', 'gy')), may hold values from 0.05 to 0.5
- seg_pressure: float32 [32, 32, 128], P(('gx', 'gy')), may hold values from -6 to 6
- seg_tracer: float32 [32, 32, 128], P(('gx', 'gy')), may hold values from -6 to 6
- beta: float32 [32, 32, 128], P(('gx', 'gy')), may hold values from 0.1 to 0.9
Outputs:
- grad_tracer: float32 [128, 64, 256], P('gx', 'gy')
- grad_perm: float32 [32, 32, 128], P(('gx', 'gy'))
The draws below stay inside these ranges and needn't reach their ends.
Inputs may be any that keep to these rules, and one draw needn't show every extreme that they name: parent[i, d, k] is at most d * 128 + k; it equals it at the roots of trees. Every row counts[i, :] holds exactly 128 in some entry.
All inputs are finite; a program needn't handle non-finite values.
Results may differ from the reference program's by a relative error of at most 0.00014.
Values sent between devices are 32-bit elements; how exact they have to be, the bound alone decides.
A program may use at most 128 MiB of HBM per device.

```python
import math
import jax
import jax.numpy as jnp

TX = 16
TY = 16
NZ = 256
SLOTS = 128
NDEV = 32
NX = 128
NY = 64
N_GY = 4


def draw_counts(key, part):
    first_key, second_key, third_key = jax.random.split(key, 3)
    base = jax.random.randint(first_key, (NDEV, NDEV), 1, SLOTS + 1)
    density = jax.random.randint(second_key, (NDEV, 1), 1, 5)
    loads = jnp.clip(base * density // 2, 1, SLOTS)
    full_owner = jax.random.randint(third_key, (NDEV,), 0, NDEV)
    column = jnp.arange(NDEV, dtype=jnp.int32)[None, :]
    loads = jnp.where(column == full_owner[:, None], SLOTS, loads)
    return loads.astype(jnp.int32)


def draw_parent(key, part):
    position = jnp.arange(NDEV * SLOTS, dtype=jnp.int32)[None, :]
    upper_bound = jnp.broadcast_to(position + 1, (NDEV, NDEV * SLOTS))
    chosen = jax.random.randint(key, (NDEV, NDEV * SLOTS), 0, upper_bound)
    return chosen.reshape(NDEV, NDEV, SLOTS).astype(jnp.int32)


def plant(array, stream_key, smallest, top_value):
    spot = [jax.random.randint(jax.random.fold_in(stream_key, axis), (), 0, length) for axis, length in enumerate(array.shape)]
    main_axis = array.shape.index(max(array.shape))
    beside = spot[:main_axis] + [(spot[main_axis] + 1) % array.shape[main_axis]] + spot[main_axis + 1:]
    return array.at[tuple(spot)].set(smallest).at[tuple(beside)].set(top_value)


def level_of(key, shape, cuts, smallest, high):
    level, own = 1.0, jax.random.fold_in(key, 6)
    for dim, blocks in cuts:
        heights = jnp.exp(jax.random.uniform(jax.random.fold_in(own, dim), (blocks,), jnp.float32, smallest / len(cuts), high / len(cuts)))
        level = level * jnp.repeat(heights, shape[dim] // blocks).reshape([-1 if axis == dim else 1 for axis in range(len(shape))])
    return level


def gaussian(key, shape, spread, limit, cuts=(), kind=jnp.bfloat16):
    array = spread * jax.random.normal(key, shape, jnp.float32)
    if cuts:
        array = array * level_of(key, shape, cuts, -0.22, 0.18)
    return jnp.clip(array, -limit, limit).astype(kind)


def setup_inputs(seed: int = 0) -> dict:
    key_of = jax.random.split(jax.random.key(seed), 14)
    return {
        "tracer": gaussian(key_of[0], (NX, NY, NZ), 1.0, 6.0, ((0, 8), (1, 4)), jnp.float32),
        "tensor": jnp.clip(jnp.exp(math.log(0.15) - 2.014903 * jax.random.uniform(key_of[1], (3, NX, NY, NZ), jnp.float32) ** level_of(key_of[1], (3, NX, NY, NZ), ((1, 8), (2, 4)), -0.2, 0.2)), 0.02, 0.15),
        "pressure": gaussian(key_of[2], (NX, NY, NZ), 1.0, 6.0, ((0, 8), (1, 4)), jnp.float32),
        "observed": gaussian(key_of[3], (NX, NY, NZ), 1.0, 6.0, ((0, 8), (1, 4)), jnp.float32),
        "depth": plant(jax.random.randint(key_of[4], (NX, NY), 0, NZ + 1), jax.random.fold_in(key_of[4], 1), 0, NZ).astype(jnp.int32),
        "cell": plant(jax.random.randint(key_of[5], (NDEV, NDEV, SLOTS), 0, TX * TY * NZ), jax.random.fold_in(key_of[5], 1), 0, (TX * TY * NZ) - 1).astype(jnp.int32),
        "parent": draw_parent(jax.random.fold_in(key_of[13], 71), 0),
        "counts": draw_counts(jax.random.fold_in(key_of[13], 71), 0),
        "perm": jnp.clip(jnp.exp(math.log(0.5) - 2.3025851 * jax.random.uniform(key_of[8], (NDEV, NDEV, SLOTS), jnp.float32) ** level_of(key_of[8], (NDEV, NDEV, SLOTS), ((0, 32),), -0.2, 0.2)), 0.05, 0.5),
        "filt": jnp.clip(jnp.exp(math.log(0.5) - 2.3025851 * jax.random.uniform(key_of[9], (NDEV, NDEV, SLOTS), jnp.float32) ** level_of(key_of[9], (NDEV, NDEV, SLOTS), ((0, 32),), -0.2, 0.2)), 0.05, 0.5),
        "seg_pressure": gaussian(key_of[10], (NDEV, NDEV, SLOTS), 1.0, 6.0, ((0, 32),), jnp.float32),
        "seg_tracer": gaussian(key_of[11], (NDEV, NDEV, SLOTS), 1.0, 6.0, ((0, 32),), jnp.float32),
        "beta": jnp.clip(jnp.exp(math.log(0.9) - 2.1972245 * jax.random.uniform(key_of[12], (NDEV, NDEV, SLOTS), jnp.float32) ** level_of(key_of[12], (NDEV, NDEV, SLOTS), ((0, 32),), -0.2, 0.2)), 0.1, 0.9),
    }


upwind_rate = 0.3

def harmonic(lower_k, upper_k):
    return 2.0 * lower_k * upper_k / (lower_k + upper_k)

def diffuse(field, tensor):
    padded = jnp.pad(field, 1)
    cond = jnp.pad(tensor, ((0, 0), (1, 1), (1, 1), (1, 1)))
    field_x = padded[:, 1:-1, 1:-1]
    cond_x = cond[0, :, 1:-1, 1:-1]
    flow_x = harmonic(cond_x[:-1], cond_x[1:]) * (field_x[1:] - field_x[:-1])
    result = flow_x[1:] - flow_x[:-1]
    field_y = padded[1:-1, :, 1:-1]
    cond_y = cond[1, 1:-1, :, 1:-1]
    flow_y = harmonic(cond_y[:, :-1], cond_y[:, 1:]) * (field_y[:, 1:] - field_y[:, :-1])
    result = result + (flow_y[:, 1:] - flow_y[:, :-1])
    field_z = padded[1:-1, 1:-1, :]
    cond_z = cond[2, 1:-1, 1:-1, :]
    flow_z = harmonic(cond_z[:, :, :-1], cond_z[:, :, 1:]) * (field_z[:, :, 1:] - field_z[:, :, :-1])
    result = result + (flow_z[:, :, 1:] - flow_z[:, :, :-1])
    return result

def reference(tracer, tensor, pressure, observed, depth, cell, parent, counts, perm, filt, seg_pressure, seg_tracer, beta):
    owner = jnp.arange(NDEV, dtype=jnp.int32)[None, :, None]
    owner_x = owner // N_GY
    owner_y = owner % N_GY
    local_x = cell // (TY * NZ)
    local_y = cell // NZ % TY
    local_z = cell % NZ
    global_index = (((owner_x * TX + local_x) * NY + (owner_y * TY + local_y)) * NZ + local_z).astype(jnp.int32)
    flat_index = global_index.reshape(-1)
    active = (jnp.arange(SLOTS, dtype=jnp.int32)[None, None, :] < counts[:, :, None]).astype(tracer.dtype)
    parent_rows = parent.reshape(NDEV, NDEV * SLOTS)
    press_at = pressure.reshape(-1)[flat_index].reshape(cell.shape)
    observed_mask = (jnp.arange(NZ, dtype=jnp.int32)[None, None, :] < depth[:, :, None]).astype(tracer.dtype)

    def misfit(start, permeab):
        tissue = start
        vessel = seg_tracer
        for ordinal in range(2):
            sampled = tissue.reshape(-1)[flat_index].reshape(cell.shape)
            flux = active * (permeab * (vessel - sampled) + filt * (seg_pressure - press_at))
            upstream = jnp.take_along_axis(vessel.reshape(NDEV, NDEV * SLOTS), parent_rows, 1).reshape(cell.shape)
            deposit = jnp.zeros_like(tissue).reshape(-1).at[flat_index].add(flux.reshape(-1)).reshape(tissue.shape)
            tissue = tissue + diffuse(tissue, tensor) + deposit
            vessel = (1.0 - upwind_rate) * vessel + upwind_rate * upstream - beta * flux
        return 0.5 * jnp.sum(observed_mask * (tissue - observed) ** 2)
    grad_tracer, grad_perm = jax.grad(misfit, argnums=(0, 1))(tracer, perm)
    return (grad_tracer, grad_perm)
```

```python
import functools

import jax
import jax.numpy as jnp
from jax import lax
from jax.experimental import pallas as pl
from jax.experimental.pallas import tpu as pltpu
from jax.sharding import PartitionSpec as P

MESH = pl.DeviceIdType.MESH
upwind_rate = 0.3
f32, bf16 = jnp.float32, jnp.bfloat16
CELL, VESSEL, CARRIED, PERM, FILT, PRESS, BETA, ACTIVE = range(8)


def harmonic(lower_k, upper_k):
    return 2.0 * lower_k * upper_k / (lower_k + upper_k)


def halves(x):
    high = x.astype(bf16)
    return high, (x - high.astype(f32)).astype(bf16)


def column_of(row, count):
    tile = jnp.broadcast_to(row, (16, row.shape[1])).astype(bf16)
    return jnp.concatenate([tile] * (count // 16), axis=0)


def one_hot(row, count):
    position = lax.broadcasted_iota(jnp.int32, (count, row.shape[1]), 0).astype(f32)
    return jnp.where(position == row, 1.0, 0.0).astype(bf16)


def kernel(
    n_gx,
    n_gy,
    tracer_in,
    tensor_in,
    pressure_in,
    observed_in,
    depth,
    cell,
    parent,
    counts,
    perm,
    filt,
    seg_pressure,
    seg_tracer,
    beta,
    out,
    out_perm,
    sent,
    fields,
    parent_hot,
    parent_group,
    carried,
    level_hot,
    column_hot,
    rows,
    field,
    added,
    total,
    face_x,
    face_y0,
    face_y1,
    face_z0,
    face_z1,
    mask,
    halo_out,
    halo_in,
    perm_out,
    perm_in,
    ex_send,
    ex_recv,
    halo_send,
    halo_recv,
    perm_send,
    perm_recv,
    load_sem,
    tracer,
    tensor,
    pressure,
    observed,
):
    n = n_gx * n_gy
    loads = [
        pltpu.make_async_copy(source, held, load_sem.at[i])
        for i, (source, held) in enumerate(
            (
                (tensor_in, tensor),
                (tracer_in, tracer),
                (pressure_in, pressure),
                (observed_in, observed),
            )
        )
    ]
    for load in loads:
        load.start()
    gx, gy = lax.axis_index("gx"), lax.axis_index("gy")
    me = gx * n_gy + gy
    tx, ty, nz = tracer.shape
    columns = tx * ty
    slots = cell.shape[2]
    width = n * slots

    barrier = pltpu.get_barrier_semaphore()

    def each_peer(body):
        @pl.loop(0, n_gx)
        def _(dx):
            x = gx + dx
            x = jnp.where(x >= n_gx, x - n_gx, x)
            for dy in range(n_gy):
                y = gy + dy
                y = jnp.where(y >= n_gy, y - n_gy, y)
                if dy:
                    body(x * n_gy + y, (x, y))
                else:

                    @pl.when(dx > 0)
                    def _(y=y):
                        body(x * n_gy + y, (x, y))

    each_peer(
        lambda d, where: pl.semaphore_signal(
            barrier, inc=1, device_id=where, device_id_type=MESH
        )
    )

    for g in range(n // 8):
        block = parent[0, 8 * g : 8 * g + 8, :]
        lane = (block & (slots - 1)).astype(f32)
        group = (block // slots).astype(f32)
        for r in range(8):
            at = (8 * g + r) * slots
            parent_hot[:, at : at + slots] = one_hot(lane[r : r + 1, :], slots)
            parent_group[:, at : at + slots] = group[r : r + 1, :]
    high, low = halves(seg_tracer[0])
    step = 1024
    for c in range(width // step):
        span = slice(c * step, (c + 1) * step)
        picked = jnp.dot(high, parent_hot[:, span], preferred_element_type=f32) + jnp.dot(
            low, parent_hot[:, span], preferred_element_type=f32
        )
        position = lax.broadcasted_iota(jnp.int32, (n, step), 0).astype(f32)
        upstream = jnp.sum(
            jnp.where(position == parent_group[:, span], picked, 0.0), axis=0, keepdims=True
        )
        carried[:, span] = upwind_rate * upstream
    live = lax.broadcasted_iota(jnp.int32, (1, slots), 1)
    for d in range(n):
        at = slice(d * slots, (d + 1) * slots)
        vessel = seg_tracer[0, d : d + 1, :]
        sent[d, CELL : CELL + 1, :] = cell[0, d : d + 1, :].astype(f32)
        sent[d, VESSEL : VESSEL + 1, :] = vessel
        sent[d, CARRIED : CARRIED + 1, :] = (1.0 - upwind_rate) * vessel + carried[:, at]
        sent[d, PERM : PERM + 1, :] = perm[0, d : d + 1, :]
        sent[d, FILT : FILT + 1, :] = filt[0, d : d + 1, :]
        sent[d, PRESS : PRESS + 1, :] = seg_pressure[0, d : d + 1, :]
        sent[d, BETA : BETA + 1, :] = beta[0, d : d + 1, :]
        sent[d, ACTIVE : ACTIVE + 1, :] = jnp.where(live < counts[0, d], 1.0, 0.0)

    has = (gx > 0, gx < n_gx - 1, gy > 0, gy < n_gy - 1)
    to = ((gx - 1, gy), (gx + 1, gy), (gx, gy - 1), (gx, gy + 1))

    def plane(x):
        return slice(x * ty, (x + 1) * ty)

    def halo_copy(phase, way):
        held = pl.ds(0, ty if phase else 2 * ty)
        return pltpu.make_async_remote_copy(
            src_ref=halo_out.at[phase, way, held],
            dst_ref=halo_in.at[phase, way ^ 1, held],
            send_sem=halo_send.at[phase, way],
            recv_sem=halo_recv.at[phase, way ^ 1],
            device_id=to[way],
            device_id_type=MESH,
        )

    def halo_arrival(phase, way):
        held = pl.ds(0, ty if phase else 2 * ty)
        return pltpu.make_async_remote_copy(
            src_ref=halo_out.at[phase, way, held],
            dst_ref=halo_in.at[phase, way, held],
            send_sem=halo_send.at[phase, way],
            recv_sem=halo_recv.at[phase, way],
            device_id=to[way],
            device_id_type=MESH,
        )

    def stage(phase, first, source):
        halo_out[phase, 0, first : first + ty, :] = source(0, 0)
        halo_out[phase, 1, first : first + ty, :] = source(0, tx - 1)
        for x in range(tx):
            held = source(1, x)
            halo_out[phase, 2, first + x : first + x + 1, :] = held[0:1, :]
            halo_out[phase, 3, first + x : first + x + 1, :] = held[ty - 1 : ty, :]

    def send_halo(phase):
        for way in range(4):

            @pl.when(has[way])
            def _(way=way):
                halo_copy(phase, way).start()

    def wait_halo(phase):
        for way in range(4):

            @pl.when(has[way])
            def _(way=way):
                halo_arrival(phase, way).wait_recv()

    loads[0].wait()
    loads[1].wait()
    stage(0, 0, lambda kind, x: tensor[kind, x])
    stage(0, ty, lambda kind, x: tracer[x])
    for way in range(4):

        @pl.when(jnp.logical_not(has[way]))
        def _(way=way):
            for phase in range(4):
                halo_in[phase, way] = jnp.zeros((2 * ty, nz), f32)

    pl.semaphore_wait(barrier, n - 1)
    send_halo(0)

    def lanes(d):
        return pl.ds(pl.multiple_of(d * slots, slots), slots)

    def exchange(d, where):
        return pltpu.make_async_remote_copy(
            src_ref=sent.at[d],
            dst_ref=fields.at[:, lanes(me)],
            send_sem=ex_send.at[d],
            recv_sem=ex_recv.at[me],
            device_id=where,
            device_id_type=MESH,
        )

    each_peer(lambda d, where: exchange(d, where).start())

    fields[:, lanes(me)] = sent[me]

    inner_y = lax.broadcasted_iota(jnp.int32, (ty, nz), 0)
    inner_z = lax.broadcasted_iota(jnp.int32, (ty, nz), 1)
    square = lax.broadcasted_iota(jnp.int32, (ty, ty), 0) == lax.broadcasted_iota(
        jnp.int32, (ty, ty), 1
    )
    for x in range(tx):
        deep = jnp.broadcast_to(depth[x : x + 1, :].astype(f32), (ty, ty))
        deep = jnp.sum(jnp.where(square, deep, 0.0), axis=1, keepdims=True)
        mask[plane(x), :] = jnp.where(inner_z.astype(f32) < deep, 1.0, 0.0)
        k = tensor[2, x]
        ahead, behind = pltpu.roll(k, nz - 1, 1), pltpu.roll(k, 1, 1)
        face_z0[plane(x), :] = jnp.where(inner_z == 0, 0.0, harmonic(behind, k))
        face_z1[plane(x), :] = jnp.where(inner_z == nz - 1, 0.0, harmonic(k, ahead))
        if x:
            face_x[plane(x), :] = harmonic(tensor[0, x - 1], tensor[0, x])
    wait_halo(0)
    face_x[plane(0), :] = harmonic(halo_in[0, 0, 0:ty, :], tensor[0, 0])
    face_x[plane(tx), :] = harmonic(tensor[0, tx - 1], halo_in[0, 1, 0:ty, :])

    def around_y(phase, first, x, value):
        before = halo_in[phase, 2, first + x : first + x + 1, :]
        after = halo_in[phase, 3, first + x : first + x + 1, :]
        behind = jnp.where(inner_y == 0, before, pltpu.roll(value, 1, 0))
        ahead = jnp.where(inner_y == ty - 1, after, pltpu.roll(value, ty - 1, 0))
        return behind, ahead

    for x in range(tx):
        k = tensor[1, x]
        behind, ahead = around_y(0, 0, x, k)
        face_y0[plane(x), :] = harmonic(behind, k)
        face_y1[plane(x), :] = harmonic(k, ahead)

    def diffused(phase, first, x):
        value = field[plane(x), :]
        below = halo_in[phase, 0, first : first + ty, :] if x == 0 else field[plane(x - 1), :]
        above = halo_in[phase, 1, first : first + ty, :] if x == tx - 1 else field[plane(x + 1), :]
        result = face_x[plane(x + 1), :] * (above - value) - face_x[plane(x), :] * (value - below)
        behind, ahead = around_y(phase, first, x, value)
        result = result + (
            face_y1[plane(x), :] * (ahead - value) - face_y0[plane(x), :] * (value - behind)
        )
        behind, ahead = pltpu.roll(value, 1, 1), pltpu.roll(value, nz - 1, 1)
        return result + (
            face_z1[plane(x), :] * (ahead - value) - face_z0[plane(x), :] * (value - behind)
        )

    for x in range(tx):
        field[plane(x), :] = tracer[x]
    for x in range(tx):
        added[plane(x), :] = tracer[x] + diffused(0, ty, x)

    together = 4

    @pl.loop(0, n // together)
    def _(c):
        for r in range(together):
            i = c * together + r

            @pl.when(i != me)
            def _(i=i):
                pltpu.make_async_remote_copy(
                    src_ref=sent.at[i],
                    dst_ref=fields.at[:, lanes(i)],
                    send_sem=ex_send.at[i],
                    recv_sem=ex_recv.at[i],
                    device_id=to[0],
                    device_id_type=MESH,
                ).wait_recv()

        span = pl.ds(pl.multiple_of(c * (together * slots), together * slots), together * slots)
        index = fields[CELL : CELL + 1, span]
        at = jnp.floor(index * (1.0 / nz))
        column_hot[:, span] = one_hot(at, columns)
        level_hot[:, span] = one_hot(index - nz * at, nz)

    chunk = min(width, 2048)

    def spans(body):
        @pl.loop(0, width // chunk)
        def _(c):
            body(pl.ds(pl.multiple_of(c * chunk, chunk), chunk))

    def sample(table, span):
        hot = level_hot[:, span]
        picked = jnp.dot(
            table, jnp.concatenate([hot, hot], axis=0), preferred_element_type=f32
        )
        picked = picked * column_hot[:, span].astype(f32)
        return jnp.sum(picked, axis=0, keepdims=True)

    def deposit(values, span):
        hot = column_hot[:, span]
        contract = (((1,), (1,)), ((), ()))
        high, low = halves(values)
        high, low = (hot * column_of(half.astype(f32), columns) for half in (high, low))
        placed = lax.dot_general(
            jnp.concatenate([high, low], axis=0),
            level_hot[:, span],
            contract,
            preferred_element_type=f32,
        )
        total[...] += placed[:columns] + placed[columns:]

    def get(name, span):
        return fields[name : name + 1, span]

    FILTERED, GAP0, GAP1, WEIGHTED, GRAD = range(5)

    def keep(name, span, value):
        rows[name : name + 1, span] = value

    def kept(name, span):
        return rows[name : name + 1, span]

    def table_of(x):
        return jnp.concatenate(halves(x), axis=1)

    loads[2].wait()
    loads[3].wait()
    table = table_of(pressure[...].reshape(columns, nz))
    first_table = table_of(field[...])
    total[...] = jnp.zeros_like(total)

    def first(span):
        filtered = get(FILT, span) * (get(PRESS, span) - sample(table, span))
        gap = get(VESSEL, span) - sample(first_table, span)
        flux = get(ACTIVE, span) * (get(PERM, span) * gap + filtered)
        keep(FILTERED, span, filtered)
        keep(GAP0, span, gap)
        keep(GAP1, span, get(CARRIED, span) - get(BETA, span) * flux)
        deposit(flux, span)

    spans(first)
    field[...] = added[...] + total[...]

    def start(phase):
        stage(phase, 0, lambda kind, x: field[plane(x), :])
        send_halo(phase)
        total[...] = jnp.zeros_like(total)

    start(1)
    second_table = table_of(field[...])

    def second(span):
        gap = kept(GAP1, span) - sample(second_table, span)
        flux = get(ACTIVE, span) * (get(PERM, span) * gap + kept(FILTERED, span))
        keep(GAP1, span, gap)
        deposit(flux, span)

    spans(second)
    wait_halo(1)
    for x in range(tx):
        tissue = field[plane(x), :] + diffused(1, 0, x) + total[plane(x), :]
        added[plane(x), :] = mask[plane(x), :] * (tissue - observed[x])
    field[...] = added[...]

    start(2)
    third_table = table_of(field[...])

    def third(span):
        adjoint = get(ACTIVE, span) * sample(third_table, span)
        keep(GRAD, span, adjoint * kept(GAP1, span))
        weighted = get(PERM, span) * adjoint
        keep(WEIGHTED, span, weighted)
        deposit(weighted, span)

    spans(third)
    wait_halo(2)
    for x in range(tx):
        added[plane(x), :] = field[plane(x), :] + diffused(2, 0, x) - total[plane(x), :]
    field[...] = added[...]

    start(3)
    fourth_table = table_of(field[...])

    def fourth(span):
        adjoint = get(ACTIVE, span) * (
            sample(fourth_table, span) - get(BETA, span) * kept(WEIGHTED, span)
        )
        keep(GRAD, span, kept(GRAD, span) + adjoint * kept(GAP0, span))
        keep(WEIGHTED, span, get(PERM, span) * adjoint)

    spans(fourth)

    for i in range(n):
        perm_out[i] = rows[GRAD : GRAD + 1, i * slots : (i + 1) * slots]

    def give(d, where):
        return pltpu.make_async_remote_copy(
            src_ref=perm_out.at[d],
            dst_ref=perm_in.at[me],
            send_sem=perm_send.at[d],
            recv_sem=perm_recv.at[me],
            device_id=where,
            device_id_type=MESH,
        )

    each_peer(lambda d, where: give(d, where).start())
    spans(lambda span: deposit(kept(WEIGHTED, span), span))
    perm_in[me] = perm_out[me]
    wait_halo(3)
    for x in range(tx):
        out[x] = field[plane(x), :] + diffused(3, 0, x) - total[plane(x), :]

    @pl.loop(0, n)
    def _(d):
        @pl.when(d != me)
        def _():
            pltpu.make_async_remote_copy(
                src_ref=perm_out.at[d],
                dst_ref=perm_in.at[d],
                send_sem=perm_send.at[d],
                recv_sem=perm_recv.at[d],
                device_id=to[0],
                device_id_type=MESH,
            ).wait()
            exchange(d, to[0]).wait_send()

    for way in range(4):

        @pl.when(has[way])
        def _(way=way):
            for phase in range(4):
                halo_copy(phase, way).wait_send()

    for d in range(n):
        out_perm[0, d : d + 1, :] = perm_in[d]


def solution(mesh):
    n_gx, n_gy = mesh.shape["gx"], mesh.shape["gy"]
    n = n_gx * n_gy

    def shards(tracer, tensor, pressure, observed, depth, cell, *rest):
        tx, ty, nz = tracer.shape
        slots = cell.shape[2]
        width, columns = n * slots, tx * ty
        vmem = pl.BlockSpec(memory_space=pltpu.VMEM)
        tile = pltpu.VMEM((columns, nz), f32)
        dma = pltpu.SemaphoreType.DMA
        return pl.pallas_call(
            functools.partial(kernel, n_gx, n_gy),
            out_shape=(
                pltpu.VMEM(tracer.shape, f32),
                pltpu.VMEM(cell.shape, f32),
            ),
            in_specs=[pl.BlockSpec(memory_space=pl.ANY)] * 4 + [vmem] * 3 + [pl.BlockSpec(memory_space=pltpu.SMEM)] + [vmem] * 5,
            out_specs=(vmem, vmem),
            scratch_shapes=[
                pltpu.VMEM((n, 8, slots), f32),
                pltpu.VMEM((8, width), f32),
                pltpu.VMEM((slots, width), bf16),
                pltpu.VMEM((1, width), f32),
                pltpu.VMEM((1, width), f32),
                pltpu.VMEM((nz, width), bf16),
                pltpu.VMEM((columns, width), bf16),
                pltpu.VMEM((8, width), f32),
                tile,
                tile,
                tile,
                pltpu.VMEM((columns + ty, nz), f32),
                tile,
                tile,
                tile,
                tile,
                tile,
                pltpu.VMEM((4, 4, 2 * ty, nz), f32),
                pltpu.VMEM((4, 4, 2 * ty, nz), f32),
                pltpu.VMEM((n, 1, slots), f32),
                pltpu.VMEM((n, 1, slots), f32),
                dma((n,)),
                dma((n,)),
                dma((4, 4)),
                dma((4, 4)),
                dma((n,)),
                dma((n,)),
                dma((4,)),
                pltpu.VMEM(tracer.shape, f32),
                pltpu.VMEM(tensor.shape, f32),
                pltpu.VMEM(tracer.shape, f32),
                pltpu.VMEM(tracer.shape, f32),
            ],
            compiler_params=pltpu.CompilerParams(
                collective_id=0, has_side_effects=True, vmem_limit_bytes=56 << 20
            ),
        )(tracer, tensor, pressure, observed, depth, cell, *rest)

    return jax.shard_map(
        shards,
        mesh=mesh,
        in_specs=(
            P("gx", "gy", None),
            P(None, "gx", "gy", None),
            P("gx", "gy", None),
            P("gx", "gy", None),
            P("gx", "gy"),
            P(("gx", "gy"), None, None),
            P(("gx", "gy"), None, None),
            P(("gx", "gy"), None),
            P(("gx", "gy"), None, None),
            P(("gx", "gy"), None, None),
            P(("gx", "gy"), None, None),
            P(("gx", "gy"), None, None),
            P(("gx", "gy"), None, None),
        ),
        out_specs=(P("gx", "gy", None), P(("gx", "gy"), None, None)),
        check_vma=False,
    )
```

```python
import functools

import jax
import jax.numpy as jnp
from jax import lax
from jax.experimental import pallas as pl
from jax.experimental.pallas import tpu as pltpu
from jax.sharding import PartitionSpec as P

MESH = pl.DeviceIdType.MESH
upwind_rate = 0.3
f32, bf16 = jnp.float32, jnp.bfloat16
CELL, VESSEL, CARRIED, PERM, FILT, DRIVE, BETA = range(7)
GAP0, AFTER, GAP1, COUPLED = range(4)


def harmonic(lower_k, upper_k):
    return 2.0 * lower_k * upper_k / (lower_k + upper_k)


def halves(x):
    high = x.astype(bf16)
    return high, (x - high.astype(f32)).astype(bf16)


def column_of(row, count):
    tile = jnp.broadcast_to(row, (16, row.shape[1])).astype(bf16)
    return jnp.concatenate([tile] * (count // 16), axis=0)


def one_hot(row, count):
    position = lax.broadcasted_iota(jnp.int32, (count, row.shape[1]), 0).astype(f32)
    return jnp.where(position == row, 1.0, 0.0).astype(bf16)


def kernel(n_gx, n_gy, *refs):
    (
        tracer_in,
        tensor_in,
        pressure_in,
        observed_in,
        depth_in,
        cell_in,
        parent_in,
        counts_in,
        perm_in_hbm,
        filt_in,
        seg_pressure_in,
        seg_tracer_in,
        beta_in,
        out,
        out_perm,
        tracer,
        tensor,
        pressure,
        observed,
        depth,
        cell,
        parent,
        counts,
        perm,
        filt,
        drive,
        seg_tracer,
        beta,
        active,
        sent,
        fields,
        parent_hot,
        parent_group,
        carried,
        level_hot,
        column_hot,
        rows,
        grad,
        table,
        field,
        second,
        base,
        total,
        face_x,
        face_y,
        face_z,
        mask,
        rim,
        rim_total,
        ghost,
        halo_out,
        halo_in,
        corner_out,
        corner_in,
        perm_back,
        ex_send,
        ex_recv,
        halo_send,
        halo_recv,
        corner_send,
        corner_recv,
        perm_send,
        perm_recv,
        load_sem,
    ) = refs
    n = n_gx * n_gy
    loads = {}
    for i, (name, source, held) in enumerate(
        (
            ("parent", parent_in, parent),
            ("vessel", seg_tracer_in, seg_tracer),
            ("counts", counts_in, counts),
            ("cell", cell_in, cell),
            ("perm", perm_in_hbm, perm),
            ("filt", filt_in, filt),
            ("drive", seg_pressure_in, drive),
            ("beta", beta_in, beta),
            ("depth", depth_in, depth),
            ("tracer", tracer_in, tracer),
            ("tensor", tensor_in, tensor),
            ("pressure", pressure_in, pressure),
            ("observed", observed_in, observed),
        )
    ):
        loads[name] = pltpu.make_async_copy(source, held, load_sem.at[i])
        loads[name].start()
    gx, gy = lax.axis_index("gx"), lax.axis_index("gy")
    me = gx * n_gy + gy
    tx, ty, nz = tracer.shape
    columns = tx * ty
    slots = cell.shape[2]
    width = n * slots

    barrier = pltpu.get_barrier_semaphore()

    def turns(value, count):
        bits = []
        for b in range(count.bit_length() - 1):
            bits.append((2**b, (1 - 2 * lax.rem(lax.div(value, 2**b), 2)) * 2**b))
        return bits

    turns_x, turns_y = turns(gx, n_gx), turns(gy, n_gy)

    def peer_x(j):
        x = gx
        for size, turn in turns_x:
            x = x + lax.rem(lax.div(j, size), 2) * turn
        return x

    peers_y = []
    for l in range(n_gy):
        y = gy
        for size, turn in turns_y:
            if l // size % 2:
                y = y + turn
        peers_y.append(y)

    def each_peer(first, last, body):
        @pl.loop(first, last)
        def _(i):
            j = n_gx - 1 - i
            x = peer_x(j)
            for l in reversed(range(n_gy)):
                y = peers_y[l]
                if l:
                    body(j * n_gy + l, x * n_gy + y, (x, y))
                else:

                    @pl.when(j > 0)
                    def _(y=y):
                        body(j * n_gy, x * n_gy + y, (x, y))

    each_peer(
        0,
        n_gx,
        lambda k, d, where: pl.semaphore_signal(
            barrier, inc=1, device_id=where, device_id_type=MESH
        ),
    )

    loads["parent"].wait()
    for g in range(n // 8):
        block = parent[0, 8 * g : 8 * g + 8, :]
        lane = (block & (slots - 1)).astype(f32)
        group = (block // slots).astype(f32)
        for r in range(8):
            at = (8 * g + r) * slots
            parent_hot[:, at : at + slots] = one_hot(lane[r : r + 1, :], slots)
            parent_group[:, at : at + slots] = group[r : r + 1, :]
    loads["vessel"].wait()
    high, low = halves(seg_tracer[0])
    step = 1024
    for c in range(width // step):
        span = slice(c * step, (c + 1) * step)
        picked = jnp.dot(high, parent_hot[:, span], preferred_element_type=f32) + jnp.dot(
            low, parent_hot[:, span], preferred_element_type=f32
        )
        position = lax.broadcasted_iota(jnp.int32, (n, step), 0).astype(f32)
        upstream = jnp.sum(
            jnp.where(position == parent_group[:, span], picked, 0.0), axis=0, keepdims=True
        )
        carried[:, span] = upwind_rate * upstream

    for name in ("counts", "cell", "perm", "filt", "drive", "beta"):
        loads[name].wait()
    diagonal = lax.broadcasted_iota(jnp.int32, (n, n), 0) == lax.broadcasted_iota(
        jnp.int32, (n, n), 1
    )
    live = jnp.broadcast_to(counts[...].astype(f32), (n, n))
    live = jnp.sum(jnp.where(diagonal, live, 0.0), axis=1, keepdims=True)
    slot = lax.broadcasted_iota(jnp.int32, (n, slots), 1).astype(f32)
    active[...] = jnp.where(slot < live, 1.0, 0.0)
    perm[0] = perm[0] * active[...]
    filt[0] = filt[0] * active[...]
    drive[0] = drive[0] * filt[0]
    for d in range(n):
        at = slice(d * slots, (d + 1) * slots)
        vessel = seg_tracer[0, d : d + 1, :]
        sent[d, CELL : CELL + 1, :] = cell[0, d : d + 1, :].astype(f32)
        sent[d, VESSEL : VESSEL + 1, :] = vessel
        sent[d, CARRIED : CARRIED + 1, :] = (1.0 - upwind_rate) * vessel + carried[:, at]
        sent[d, PERM : PERM + 1, :] = perm[0, d : d + 1, :]
        sent[d, FILT : FILT + 1, :] = filt[0, d : d + 1, :]
        sent[d, DRIVE : DRIVE + 1, :] = drive[0, d : d + 1, :]
        sent[d, BETA : BETA + 1, :] = beta[0, d : d + 1, :]
        sent[d, BETA + 1 : BETA + 2, :] = jnp.zeros((1, slots), f32)

    has = (gx > 0, gx < n_gx - 1, gy > 0, gy < n_gy - 1)
    to = ((gx - 1, gy), (gx + 1, gy), (gx, gy - 1), (gx, gy + 1))
    held_rows = (3 * ty, 2 * ty + 8, ty)

    def plane(x):
        return slice(x * ty, (x + 1) * ty)

    def halo_copy(phase, way, landing):
        held = pl.ds(0, held_rows[phase])
        return pltpu.make_async_remote_copy(
            src_ref=halo_out.at[phase, way, held],
            dst_ref=halo_in.at[phase, landing, held],
            send_sem=halo_send.at[phase, way],
            recv_sem=halo_recv.at[phase, landing],
            device_id=to[way],
            device_id_type=MESH,
        )

    def on_ways(body):
        for way in range(4):

            @pl.when(has[way])
            def _(way=way):
                body(way)

    def send_halo(phase):
        on_ways(lambda way: halo_copy(phase, way, way ^ 1).start())

    def wait_halo(phase):
        on_ways(lambda way: halo_copy(phase, way, way).wait_recv())

    beside = [(sx, sy) for sx in (0, 1) for sy in (0, 1)]

    def corner_copy(c, landing):
        sx, sy = beside[c]
        return pltpu.make_async_remote_copy(
            src_ref=corner_out.at[c],
            dst_ref=corner_in.at[landing],
            send_sem=corner_send.at[c],
            recv_sem=corner_recv.at[landing],
            device_id=(gx + 2 * sx - 1, gy + 2 * sy - 1),
            device_id_type=MESH,
        )

    def on_corners(body):
        for c, (sx, sy) in enumerate(beside):

            @pl.when(jnp.logical_and(has[sx], has[2 + sy]))
            def _(c=c):
                body(c)

    def stage(phase, first, source):
        halo_out[phase, 0, first : first + ty, :] = source(0, 0)
        halo_out[phase, 1, first : first + ty, :] = source(0, tx - 1)
        for x in range(tx):
            held = source(1, x)
            halo_out[phase, 2, first + x : first + x + 1, :] = held[0:1, :]
            halo_out[phase, 3, first + x : first + x + 1, :] = held[ty - 1 : ty, :]

    inner_y = lax.broadcasted_iota(jnp.int32, (ty, nz), 0)
    inner_z = lax.broadcasted_iota(jnp.int32, (ty, nz), 1)
    square = lax.broadcasted_iota(jnp.int32, (ty, ty), 0) == lax.broadcasted_iota(
        jnp.int32, (ty, ty), 1
    )
    for way in range(4):

        @pl.when(jnp.logical_not(has[way]))
        def _(way=way):
            for phase in range(3):
                halo_in[phase, way] = jnp.zeros((3 * ty, nz), f32)

    for c, (sx, sy) in enumerate(beside):

        @pl.when(jnp.logical_not(jnp.logical_and(has[sx], has[2 + sy])))
        def _(c=c):
            corner_in[c] = jnp.zeros((1, nz), f32)

    def lanes(k):
        return pl.ds(pl.multiple_of(k * slots, slots), slots)

    together = 8
    small = together * slots

    def exchange(k, d, where):
        return pltpu.make_async_remote_copy(
            src_ref=sent.at[d],
            dst_ref=fields.at[:, lanes(k)],
            send_sem=ex_send.at[0],
            recv_sem=ex_recv.at[lax.div(k, together)],
            device_id=where,
            device_id_type=MESH,
        )

    pl.semaphore_wait(barrier, n - 1)
    each_peer(0, n_gx, lambda k, d, where: exchange(k, d, where).start())
    fields[:, 0:slots] = sent[me]
    loads["depth"].wait()
    for x in range(tx):
        deep = jnp.broadcast_to(depth[x : x + 1, :].astype(f32), (ty, ty))
        deep = jnp.sum(jnp.where(square, deep, 0.0), axis=1, keepdims=True)
        mask[plane(x), :] = jnp.where(inner_z.astype(f32) < deep, 1.0, 0.0)
    loads["tracer"].wait()
    loads["tensor"].wait()
    stage(0, 0, lambda kind, x: tensor[kind, x])
    stage(0, ty, lambda kind, x: tracer[x])
    stage(0, 2 * ty, lambda kind, x: mask[plane(x), :])
    send_halo(0)

    for x in range(tx):
        k = tensor[2, x]
        face_z[plane(x), :] = jnp.where(inner_z == nz - 1, 0.0, harmonic(k, pltpu.roll(k, nz - 1, 1)))
        k = tensor[1, x]
        face_y[plane(x), :] = jnp.where(inner_y == ty - 1, 0.0, harmonic(k, pltpu.roll(k, ty - 1, 0)))
        if x:
            face_x[plane(x), :] = harmonic(tensor[0, x - 1], tensor[0, x])

    def spread(read, x):
        value = read(x)
        flow = face_y[plane(x), :] * (pltpu.roll(value, ty - 1, 0) - value)
        result = flow - pltpu.roll(flow, 1, 0)
        flow = face_z[plane(x), :] * (pltpu.roll(value, nz - 1, 1) - value)
        result = result + (flow - pltpu.roll(flow, 1, 1))
        if x:
            result = result - face_x[plane(x), :] * (value - read(x - 1))
        if x < tx - 1:
            result = result + face_x[plane(x + 1), :] * (read(x + 1) - value)
        return result

    def correct(target, own, beyond):
        for way in range(2):
            at = plane(way * (tx - 1))
            target[at, :] += rim[way] * (beyond(way) - own(way))
        for way in range(2, 4):
            extra = rim[way] * (beyond(way) - own(way))
            for x in range(tx):
                at = x * ty + (way - 2) * (ty - 1)
                target[at : at + 1, :] += extra[x : x + 1, :]

    def own_of(phase, first=0):
        return lambda way: halo_out[phase, way, first : first + ty, :]

    def beyond_of(phase, first=0):
        return lambda way: halo_in[phase, way, first : first + ty, :]

    for x in range(tx):
        base[plane(x), :] = tracer[x] + spread(lambda x: tracer[x], x)

    def fill_table(first, read):
        high, low = halves(read)
        table[first * columns : (first + 1) * columns, 0:nz] = high
        table[first * columns : (first + 1) * columns, nz : 2 * nz] = low

    loads["pressure"].wait()
    fill_table(0, pressure[...].reshape(columns, nz))
    fill_table(1, tracer[...].reshape(columns, nz))

    def sample(count, span):
        hot = level_hot[:, span]
        picked = jnp.dot(
            table[0 : count * columns, :],
            jnp.concatenate([hot, hot], axis=0),
            preferred_element_type=f32,
        )
        chosen = column_hot[:, span].astype(f32)
        return [
            jnp.sum(picked[i * columns : (i + 1) * columns] * chosen, axis=0, keepdims=True)
            for i in range(count)
        ]

    def deposit(first, values, span):
        hot = column_hot[:, span]
        contract = (((1,), (1,)), ((), ()))
        placed = lax.dot_general(
            jnp.concatenate(
                [
                    hot * column_of(half.astype(f32), columns)
                    for value in values
                    for half in halves(value)
                ],
                axis=0,
            ),
            level_hot[:, span],
            contract,
            preferred_element_type=f32,
        )
        for i in range(len(values)):
            at = 2 * i * columns
            total[first + i] += placed[at : at + columns] + placed[at + columns : at + 2 * columns]

    def get(name, span):
        return fields[name : name + 1, span]

    def keep(name, span, value):
        rows[name : name + 1, span] = value

    def kept(name, span):
        return rows[name : name + 1, span]

    total[...] = jnp.zeros_like(total)
    rim_total[...] = jnp.zeros_like(rim_total)
    place = lax.broadcasted_iota(jnp.int32, (4 * ty, small), 0).astype(f32)
    rim_column = jnp.where(
        place < 2 * ty,
        jnp.where(place < ty, place, place + (columns - 2 * ty)),
        jnp.where(place < 3 * ty, (place - 2 * ty) * ty, (place - 3 * ty) * ty + (ty - 1)),
    )
    @pl.loop(0, n // together)
    def _(c):
        @pl.when(c == n // together - 1)
        def _():
            wait_halo(0)
            for way in range(4):
                rim[way] = harmonic(halo_in[0, way, 0:ty, :], halo_out[0, way, 0:ty, :])
            for way in range(4):
                across = 2 - way // 2 * 2
                at = way % 2 * (ty - 1)
                for side in range(2):
                    halo_out[1, way, 2 * ty + side : 2 * ty + side + 1, :] = rim[
                        across + side, at : at + 1, :
                    ]
                halo_out[1, way, 2 * ty + 2 : 2 * ty + 8, :] = jnp.zeros((6, nz), f32)
            correct(base, own_of(0, ty), beyond_of(0, ty))

        span = pl.ds(pl.multiple_of(c * small, small), small)

        def arrived(landed):
            pltpu.make_async_remote_copy(
                src_ref=landed,
                dst_ref=landed,
                send_sem=ex_send.at[0],
                recv_sem=ex_recv.at[c],
                device_id=to[0],
                device_id_type=MESH,
            ).wait_recv()

        pl.when(c == 0)(lambda: arrived(fields.at[:, slots:small]))
        pl.when(c > 0)(lambda: arrived(fields.at[:, span]))
        index = get(CELL, span)
        at = jnp.floor(index * (1.0 / nz))
        column_hot[:, span] = one_hot(at, columns)
        level_hot[:, span] = one_hot(index - nz * at, nz)
        press, start = sample(2, span)
        filtered = get(DRIVE, span) - get(FILT, span) * press
        gap = get(VESSEL, span) - start
        flux = get(PERM, span) * gap + filtered
        after = get(CARRIED, span) - get(BETA, span) * flux
        keep(GAP0, span, gap)
        keep(AFTER, span, after)
        keep(COUPLED, span, press)
        perm_here = get(PERM, span)
        edge = jnp.where(rim_column == at, 1.0, 0.0).astype(bf16)
        placed = lax.dot_general(
            jnp.concatenate(
                [column_hot[:, span] * column_of(half.astype(f32), columns) for half in halves(flux)]
                + [
                    edge * column_of(half.astype(f32), 4 * ty)
                    for value in (perm_here * after + filtered, perm_here)
                    for half in halves(value)
                ],
                axis=0,
            ),
            level_hot[:, span],
            (((1,), (1,)), ((), ())),
            preferred_element_type=f32,
        )
        total[0] += placed[0:columns] + placed[columns : 2 * columns]
        for i in range(2):
            first = 2 * columns + 8 * ty * i
            rim_total[i] += placed[first : first + 4 * ty] + placed[first + 4 * ty : first + 8 * ty]

    chunk = min(width, 2048)

    for x in range(tx):
        field[plane(x), :] = base[plane(x), :] + total[0, plane(x), :]
    stage(1, 0, lambda kind, x: field[plane(x), :])
    for c, (sx, sy) in enumerate(beside):
        at = sx * (tx - 1) * ty + sy * (ty - 1)
        corner_out[c] = field[at : at + 1, :]
    on_corners(lambda c: corner_copy(c, 3 - c).start())
    loads["observed"].wait()
    for x in range(tx):
        value = field[plane(x), :]
        second[plane(x), :] = (
            value
            + spread(lambda x: field[plane(x), :], x)
            - observed[x]
        )
    stage(1, ty, lambda kind, x: second[plane(x), :])
    for way in range(4):
        at = slice(way * ty, (way + 1) * ty)
        halo_out[1, way, ty : 2 * ty, :] += (
            rim_total[0, at, :] - rim_total[1, at, :] * halo_out[1, way, 0:ty, :]
        )
    send_halo(1)

    fill_table(0, field[...])

    @pl.loop(0, width // chunk)
    def _(c):
        span = pl.ds(pl.multiple_of(c * chunk, chunk), chunk)
        (middle,) = sample(1, span)
        perm_here = get(PERM, span)
        after = kept(AFTER, span)
        filtered = get(DRIVE, span) - get(FILT, span) * kept(COUPLED, span)
        keep(COUPLED, span, get(BETA, span) * perm_here)
        keep(GAP1, span, after - middle)
        deposit(1, [perm_here * after + filtered, perm_here], span)

    wait_halo(1)
    on_corners(lambda c: corner_copy(c, c).wait_recv())
    correct(second, own_of(1), beyond_of(1))
    for x in range(tx):
        second[plane(x), :] = mask[plane(x), :] * (
            second[plane(x), :]
            + (total[1, plane(x), :] - total[2, plane(x), :] * field[plane(x), :])
        )
    for way in range(4):
        outer = halo_in[1, way, 0:ty, :]
        value = halo_in[1, way, ty : 2 * ty, :] + rim[way] * (halo_out[1, way, 0:ty, :] - outer)
        for side in range(2):
            c = 2 * (way % 2) + side if way < 2 else 2 * side + way % 2
            edge = halo_in[1, way, 2 * ty + side : 2 * ty + side + 1, :] * (corner_in[c] - outer)
            value = value + jnp.where(inner_y == side * (ty - 1), edge, 0.0)
        ghost[way] = halo_in[0, way, 2 * ty : 3 * ty, :] * value
    stage(3, 0, lambda kind, x: second[plane(x), :])
    for x in range(tx):
        value = second[plane(x), :]
        field[plane(x), :] = (
            value + spread(lambda x: second[plane(x), :], x) - total[2, plane(x), :] * value
        )
    correct(field, own_of(3), lambda way: ghost[way])
    stage(2, 0, lambda kind, x: field[plane(x), :])
    send_halo(2)

    def give(k, d, where):
        return pltpu.make_async_remote_copy(
            src_ref=grad.at[:, lanes(k)],
            dst_ref=perm_back.at[me],
            send_sem=perm_send.at[0],
            recv_sem=perm_recv.at[0],
            device_id=where,
            device_id_type=MESH,
        )

    fill_table(0, second[...])
    fill_table(1, field[...])
    parts = width // chunk
    groups = n_gx // parts

    @pl.loop(0, parts)
    def _(i):
        span = pl.ds(pl.multiple_of((parts - 1 - i) * chunk, chunk), chunk)
        late, early = sample(2, span)
        grad[:, span] = (
            late * kept(GAP1, span) + (early - kept(COUPLED, span) * late) * kept(GAP0, span)
        )
        each_peer(i * groups, (i + 1) * groups, lambda k, d, where: give(k, d, where).start())

    perm_back[me] = grad[:, 0:slots]

    @pl.loop(0, parts)
    def _(c):
        span = pl.ds(pl.multiple_of(c * chunk, chunk), chunk)
        deposit(3, [kept(COUPLED, span) * get(PERM, span)], span)

    for x in range(tx):
        value = field[plane(x), :]
        base[plane(x), :] = (
            value
            + spread(lambda x: field[plane(x), :], x)
            - total[2, plane(x), :] * value
            + total[3, plane(x), :] * second[plane(x), :]
        )
    wait_halo(2)
    correct(base, own_of(2), beyond_of(2))
    for x in range(tx):
        out[x] = base[plane(x), :]

    sent_all = sent.at[0 : n - 1]
    pltpu.make_async_remote_copy(
        src_ref=sent_all,
        dst_ref=sent_all,
        send_sem=ex_send.at[0],
        recv_sem=ex_recv.at[0],
        device_id=to[0],
        device_id_type=MESH,
    ).wait_send()
    for phase in range(3):
        on_ways(lambda way: halo_copy(phase, way, way ^ 1).wait_send())
    on_corners(lambda c: corner_copy(c, 3 - c).wait_send())
    perm_all = perm_back.at[0 : n - 1]
    pltpu.make_async_remote_copy(
        src_ref=perm_all,
        dst_ref=perm_all,
        send_sem=perm_send.at[0],
        recv_sem=perm_recv.at[0],
        device_id=to[0],
        device_id_type=MESH,
    ).wait()
    for d in range(n):
        out_perm[0, d : d + 1, :] = perm_back[d] * active[d : d + 1, :]


def solution(mesh):
    n_gx, n_gy = mesh.shape["gx"], mesh.shape["gy"]
    n = n_gx * n_gy

    def shards(tracer, tensor, pressure, observed, depth, cell, *rest):
        tx, ty, nz = tracer.shape
        slots = cell.shape[2]
        width, columns = n * slots, tx * ty
        vmem = pl.BlockSpec(memory_space=pltpu.VMEM)
        tile = pltpu.VMEM((columns, nz), f32)
        block = pltpu.VMEM(cell.shape, f32)
        ints = pltpu.VMEM(cell.shape, jnp.int32)
        dma = pltpu.SemaphoreType.DMA
        return pl.pallas_call(
            functools.partial(kernel, n_gx, n_gy),
            out_shape=(
                pltpu.VMEM(tracer.shape, f32),
                pltpu.VMEM(cell.shape, f32),
            ),
            in_specs=[pl.BlockSpec(memory_space=pl.ANY)] * 13,
            out_specs=(vmem, vmem),
            scratch_shapes=[
                pltpu.VMEM(tracer.shape, f32),
                pltpu.VMEM(tensor.shape, f32),
                pltpu.VMEM(tracer.shape, f32),
                pltpu.VMEM(tracer.shape, f32),
                pltpu.VMEM(depth.shape, jnp.int32),
                ints,
                ints,
                pltpu.VMEM((1, n), jnp.int32),
                block,
                block,
                block,
                block,
                block,
                pltpu.VMEM((n, slots), f32),
                pltpu.VMEM((n, 8, slots), f32),
                pltpu.VMEM((8, width), f32),
                pltpu.VMEM((slots, width), bf16),
                pltpu.VMEM((1, width), f32),
                pltpu.VMEM((1, width), f32),
                pltpu.VMEM((nz, width), bf16),
                pltpu.VMEM((columns, width), bf16),
                pltpu.VMEM((8, width), f32),
                pltpu.VMEM((1, width), f32),
                pltpu.VMEM((2 * columns, 2 * nz), bf16),
                tile,
                tile,
                tile,
                pltpu.VMEM((4, columns, nz), f32),
                tile,
                tile,
                tile,
                tile,
                pltpu.VMEM((4, ty, nz), f32),
                pltpu.VMEM((2, 4 * ty, nz), f32),
                pltpu.VMEM((4, ty, nz), f32),
                pltpu.VMEM((4, 4, 3 * ty, nz), f32),
                pltpu.VMEM((3, 4, 3 * ty, nz), f32),
                pltpu.VMEM((4, 1, nz), f32),
                pltpu.VMEM((4, 1, nz), f32),
                pltpu.VMEM((n, 1, slots), f32),
                dma((1,)),
                dma((n // 8,)),
                dma((3, 4)),
                dma((3, 4)),
                dma((4,)),
                dma((4,)),
                dma((1,)),
                dma((1,)),
                dma((13,)),
            ],
            compiler_params=pltpu.CompilerParams(
                collective_id=0, has_side_effects=True, vmem_limit_bytes=56 << 20
            ),
        )(tracer, tensor, pressure, observed, depth, cell, *rest)

    return jax.shard_map(
        shards,
        mesh=mesh,
        in_specs=(
            P("gx", "gy", None),
            P(None, "gx", "gy", None),
            P("gx", "gy", None),
            P("gx", "gy", None),
            P("gx", "gy"),
            P(("gx", "gy"), None, None),
            P(("gx", "gy"), None, None),
            P(("gx", "gy"), None),
            P(("gx", "gy"), None, None),
            P(("gx", "gy"), None, None),
            P(("gx", "gy"), None, None),
            P(("gx", "gy"), None, None),
            P(("gx", "gy"), None, None),
        ),
        out_specs=(P("gx", "gy", None), P(("gx", "gy"), None, None)),
        check_vma=False,
    )
```

```python
import functools

import jax
import jax.numpy as jnp
from jax import lax
from jax.experimental import pallas as pl
from jax.experimental.pallas import tpu as pltpu
from jax.sharding import PartitionSpec as P

MESH = pl.DeviceIdType.MESH
upwind_rate = 0.3
f32, bf16 = jnp.float32, jnp.bfloat16
CELL, VESSEL, CARRIED, PERM, FILT, DRIVE, BETA = range(7)
GAP0, AFTER, GAP1, COUPLED = range(4)


def harmonic(lower_k, upper_k):
    return 2.0 * lower_k * upper_k / (lower_k + upper_k)


def halves(x):
    high = x.astype(bf16)
    return high, (x - high.astype(f32)).astype(bf16)


def column_of(row, count):
    tile = jnp.broadcast_to(row, (16, row.shape[1])).astype(bf16)
    return jnp.concatenate([tile] * (count // 16), axis=0)


def one_hot(row, count):
    position = lax.broadcasted_iota(jnp.int32, (count, row.shape[1]), 0).astype(f32)
    return jnp.where(position == row, 1.0, 0.0).astype(bf16)


def kernel(n_gx, n_gy, *refs):
    (
        tracer_in,
        tensor_in,
        pressure_in,
        observed_in,
        depth_in,
        cell_in,
        parent_in,
        counts_in,
        perm_in_hbm,
        filt_in,
        seg_pressure_in,
        seg_tracer_in,
        beta_in,
        out,
        out_perm,
        tracer,
        tensor,
        pressure,
        observed,
        depth,
        cell,
        parent,
        counts,
        perm,
        filt,
        drive,
        seg_tracer,
        beta,
        active,
        sent,
        fields,
        parent_hot,
        parent_group,
        carried,
        level_hot,
        column_hot,
        rows,
        grad,
        table,
        field,
        second,
        base,
        total,
        face_x,
        face_y,
        face_z,
        mask,
        rim,
        rim_total,
        ghost,
        halo_out,
        halo_in,
        corner_out,
        corner_in,
        perm_back,
        ex_send,
        ex_recv,
        halo_send,
        halo_recv,
        corner_send,
        corner_recv,
        perm_send,
        perm_recv,
        load_sem,
    ) = refs
    n = n_gx * n_gy
    loads = {}
    for i, (name, source, held) in enumerate(
        (
            ("parent", parent_in, parent),
            ("vessel", seg_tracer_in, seg_tracer),
            ("counts", counts_in, counts),
            ("cell", cell_in, cell),
            ("perm", perm_in_hbm, perm),
            ("filt", filt_in, filt),
            ("drive", seg_pressure_in, drive),
            ("beta", beta_in, beta),
            ("depth", depth_in, depth),
            ("tracer", tracer_in, tracer),
            ("tensor", tensor_in, tensor),
            ("pressure", pressure_in, pressure),
            ("observed", observed_in, observed),
        )
    ):
        loads[name] = pltpu.make_async_copy(source, held, load_sem.at[i])
        loads[name].start()
    gx, gy = lax.axis_index("gx"), lax.axis_index("gy")
    me = gx * n_gy + gy
    tx, ty, nz = tracer.shape
    columns = tx * ty
    slots = cell.shape[2]
    width = n * slots

    barrier = pltpu.get_barrier_semaphore()

    def turns(value, count):
        bits = []
        for b in range(count.bit_length() - 1):
            bits.append((2**b, (1 - 2 * lax.rem(lax.div(value, 2**b), 2)) * 2**b))
        return bits

    turns_x, turns_y = turns(gx, n_gx), turns(gy, n_gy)

    def peer_x(j):
        x = gx
        for size, turn in turns_x:
            x = x + lax.rem(lax.div(j, size), 2) * turn
        return x

    peers_y = []
    for l in range(n_gy):
        y = gy
        for size, turn in turns_y:
            if l // size % 2:
                y = y + turn
        peers_y.append(y)

    def each_peer(first, last, body):
        @pl.loop(first, last)
        def _(i):
            j = n_gx - 1 - i
            x = peer_x(j)
            for l in reversed(range(n_gy)):
                y = peers_y[l]
                if l:
                    body(j * n_gy + l, x * n_gy + y, (x, y))
                else:

                    @pl.when(j > 0)
                    def _(y=y):
                        body(j * n_gy, x * n_gy + y, (x, y))

    each_peer(
        0,
        n_gx,
        lambda k, d, where: pl.semaphore_signal(
            barrier, inc=1, device_id=where, device_id_type=MESH
        ),
    )

    loads["parent"].wait()
    for g in range(n // 8):
        block = parent[0, 8 * g : 8 * g + 8, :]
        lane = (block & (slots - 1)).astype(f32)
        group = (block // slots).astype(f32)
        for r in range(8):
            at = (8 * g + r) * slots
            parent_hot[:, at : at + slots] = one_hot(lane[r : r + 1, :], slots)
            parent_group[:, at : at + slots] = group[r : r + 1, :]
    loads["vessel"].wait()
    high, low = halves(seg_tracer[0])
    step = 1024
    for c in range(width // step):
        span = slice(c * step, (c + 1) * step)
        picked = jnp.dot(high, parent_hot[:, span], preferred_element_type=f32) + jnp.dot(
            low, parent_hot[:, span], preferred_element_type=f32
        )
        position = lax.broadcasted_iota(jnp.int32, (n, step), 0).astype(f32)
        upstream = jnp.sum(
            jnp.where(position == parent_group[:, span], picked, 0.0), axis=0, keepdims=True
        )
        carried[:, span] = upwind_rate * upstream

    for name in ("counts", "cell", "perm", "filt", "drive", "beta"):
        loads[name].wait()
    diagonal = lax.broadcasted_iota(jnp.int32, (n, n), 0) == lax.broadcasted_iota(
        jnp.int32, (n, n), 1
    )
    live = jnp.broadcast_to(counts[...].astype(f32), (n, n))
    live = jnp.sum(jnp.where(diagonal, live, 0.0), axis=1, keepdims=True)
    slot = lax.broadcasted_iota(jnp.int32, (n, slots), 1).astype(f32)
    active[...] = jnp.where(slot < live, 1.0, 0.0)
    perm[0] = perm[0] * active[...]
    filt[0] = filt[0] * active[...]
    drive[0] = drive[0] * filt[0]
    for d in range(n):
        at = slice(d * slots, (d + 1) * slots)
        vessel = seg_tracer[0, d : d + 1, :]
        sent[d, CELL : CELL + 1, :] = cell[0, d : d + 1, :].astype(f32)
        sent[d, VESSEL : VESSEL + 1, :] = vessel
        sent[d, CARRIED : CARRIED + 1, :] = (1.0 - upwind_rate) * vessel + carried[:, at]
        sent[d, PERM : PERM + 1, :] = perm[0, d : d + 1, :]
        sent[d, FILT : FILT + 1, :] = filt[0, d : d + 1, :]
        sent[d, DRIVE : DRIVE + 1, :] = drive[0, d : d + 1, :]
        sent[d, BETA : BETA + 1, :] = beta[0, d : d + 1, :]
        sent[d, BETA + 1 : BETA + 2, :] = jnp.zeros((1, slots), f32)

    has = (gx > 0, gx < n_gx - 1, gy > 0, gy < n_gy - 1)
    to = ((gx - 1, gy), (gx + 1, gy), (gx, gy - 1), (gx, gy + 1))
    held_rows = (3 * ty, 2 * ty + 8, ty)

    def plane(x):
        return slice(x * ty, (x + 1) * ty)

    def halo_copy(phase, way, landing):
        held = pl.ds(0, held_rows[phase])
        return pltpu.make_async_remote_copy(
            src_ref=halo_out.at[phase, way, held],
            dst_ref=halo_in.at[phase, landing, held],
            send_sem=halo_send.at[phase, way],
            recv_sem=halo_recv.at[phase, landing],
            device_id=to[way],
            device_id_type=MESH,
        )

    def on_ways(body):
        for way in range(4):

            @pl.when(has[way])
            def _(way=way):
                body(way)

    def send_halo(phase):
        on_ways(lambda way: halo_copy(phase, way, way ^ 1).start())

    def wait_halo(phase):
        on_ways(lambda way: halo_copy(phase, way, way).wait_recv())

    beside = [(sx, sy) for sx in (0, 1) for sy in (0, 1)]

    def corner_copy(c, landing):
        sx, sy = beside[c]
        return pltpu.make_async_remote_copy(
            src_ref=corner_out.at[c],
            dst_ref=corner_in.at[landing],
            send_sem=corner_send.at[c],
            recv_sem=corner_recv.at[landing],
            device_id=(gx + 2 * sx - 1, gy + 2 * sy - 1),
            device_id_type=MESH,
        )

    def on_corners(body):
        for c, (sx, sy) in enumerate(beside):

            @pl.when(jnp.logical_and(has[sx], has[2 + sy]))
            def _(c=c):
                body(c)

    def stage(phase, first, source):
        halo_out[phase, 0, first : first + ty, :] = source(0, 0)
        halo_out[phase, 1, first : first + ty, :] = source(0, tx - 1)
        for x in range(tx):
            held = source(1, x)
            halo_out[phase, 2, first + x : first + x + 1, :] = held[0:1, :]
            halo_out[phase, 3, first + x : first + x + 1, :] = held[ty - 1 : ty, :]

    inner_y = lax.broadcasted_iota(jnp.int32, (ty, nz), 0)
    inner_z = lax.broadcasted_iota(jnp.int32, (ty, nz), 1)
    square = lax.broadcasted_iota(jnp.int32, (ty, ty), 0) == lax.broadcasted_iota(
        jnp.int32, (ty, ty), 1
    )
    for way in range(4):

        @pl.when(jnp.logical_not(has[way]))
        def _(way=way):
            for phase in range(3):
                halo_in[phase, way] = jnp.zeros((3 * ty, nz), f32)

    for c, (sx, sy) in enumerate(beside):

        @pl.when(jnp.logical_not(jnp.logical_and(has[sx], has[2 + sy])))
        def _(c=c):
            corner_in[c] = jnp.zeros((1, nz), f32)

    def lanes(k):
        return pl.ds(pl.multiple_of(k * slots, slots), slots)

    together = 8
    small = together * slots

    def exchange(k, d, where):
        return pltpu.make_async_remote_copy(
            src_ref=sent.at[d],
            dst_ref=fields.at[:, lanes(k)],
            send_sem=ex_send.at[0],
            recv_sem=ex_recv.at[lax.div(k, together)],
            device_id=where,
            device_id_type=MESH,
        )

    pl.semaphore_wait(barrier, n - 1)
    each_peer(0, n_gx, lambda k, d, where: exchange(k, d, where).start())
    fields[:, 0:slots] = sent[me]
    loads["depth"].wait()
    for x in range(tx):
        deep = jnp.broadcast_to(depth[x : x + 1, :].astype(f32), (ty, ty))
        deep = jnp.sum(jnp.where(square, deep, 0.0), axis=1, keepdims=True)
        mask[plane(x), :] = jnp.where(inner_z.astype(f32) < deep, 1.0, 0.0)
    loads["tracer"].wait()
    loads["tensor"].wait()
    stage(0, 0, lambda kind, x: tensor[kind, x])
    stage(0, ty, lambda kind, x: tracer[x])
    stage(0, 2 * ty, lambda kind, x: mask[plane(x), :])
    send_halo(0)

    for x in range(tx):
        k = tensor[2, x]
        face_z[plane(x), :] = jnp.where(inner_z == nz - 1, 0.0, harmonic(k, pltpu.roll(k, nz - 1, 1)))
        k = tensor[1, x]
        face_y[plane(x), :] = jnp.where(inner_y == ty - 1, 0.0, harmonic(k, pltpu.roll(k, ty - 1, 0)))
        if x:
            face_x[plane(x), :] = harmonic(tensor[0, x - 1], tensor[0, x])

    def spread(read, x):
        value = read(x)
        flow = face_y[plane(x), :] * (pltpu.roll(value, ty - 1, 0) - value)
        result = flow - pltpu.roll(flow, 1, 0)
        flow = face_z[plane(x), :] * (pltpu.roll(value, nz - 1, 1) - value)
        result = result + (flow - pltpu.roll(flow, 1, 1))
        if x:
            result = result - face_x[plane(x), :] * (value - read(x - 1))
        if x < tx - 1:
            result = result + face_x[plane(x + 1), :] * (read(x + 1) - value)
        return result

    def correct(target, own, beyond):
        for way in range(2):
            at = plane(way * (tx - 1))
            target[at, :] += rim[way] * (beyond(way) - own(way))
        for way in range(2, 4):
            extra = rim[way] * (beyond(way) - own(way))
            for x in range(tx):
                at = x * ty + (way - 2) * (ty - 1)
                target[at : at + 1, :] += extra[x : x + 1, :]

    def own_of(phase, first=0):
        return lambda way: halo_out[phase, way, first : first + ty, :]

    def beyond_of(phase, first=0):
        return lambda way: halo_in[phase, way, first : first + ty, :]

    for x in range(tx):
        base[plane(x), :] = tracer[x] + spread(lambda x: tracer[x], x)

    def fill_table(first, read):
        high, low = halves(read)
        table[first * columns : (first + 1) * columns, 0:nz] = high
        table[first * columns : (first + 1) * columns, nz : 2 * nz] = low

    loads["pressure"].wait()
    fill_table(0, pressure[...].reshape(columns, nz))
    fill_table(1, tracer[...].reshape(columns, nz))

    def sample(count, span):
        hot = level_hot[:, span]
        picked = jnp.dot(
            table[0 : count * columns, :],
            jnp.concatenate([hot, hot], axis=0),
            preferred_element_type=f32,
        )
        chosen = column_hot[:, span].astype(f32)
        return [
            jnp.sum(picked[i * columns : (i + 1) * columns] * chosen, axis=0, keepdims=True)
            for i in range(count)
        ]

    def deposit(first, values, span):
        hot = column_hot[:, span]
        contract = (((1,), (1,)), ((), ()))
        placed = lax.dot_general(
            jnp.concatenate(
                [
                    hot * column_of(half.astype(f32), columns)
                    for value in values
                    for half in halves(value)
                ],
                axis=0,
            ),
            level_hot[:, span],
            contract,
            preferred_element_type=f32,
        )
        for i in range(len(values)):
            at = 2 * i * columns
            total[first + i] += placed[at : at + columns] + placed[at + columns : at + 2 * columns]

    def get(name, span):
        return fields[name : name + 1, span]

    def keep(name, span, value):
        rows[name : name + 1, span] = value

    def kept(name, span):
        return rows[name : name + 1, span]

    total[...] = jnp.zeros_like(total)
    rim_total[...] = jnp.zeros_like(rim_total)
    place = lax.broadcasted_iota(jnp.int32, (4 * ty, small), 0).astype(f32)
    rim_column = jnp.where(
        place < 2 * ty,
        jnp.where(place < ty, place, place + (columns - 2 * ty)),
        jnp.where(place < 3 * ty, (place - 2 * ty) * ty, (place - 3 * ty) * ty + (ty - 1)),
    )
    @pl.loop(0, n // together)
    def _(c):
        @pl.when(c == n // together - 1)
        def _():
            wait_halo(0)
            for way in range(4):
                rim[way] = harmonic(halo_in[0, way, 0:ty, :], halo_out[0, way, 0:ty, :])
            for way in range(4):
                across = 2 - way // 2 * 2
                at = way % 2 * (ty - 1)
                for side in range(2):
                    halo_out[1, way, 2 * ty + side : 2 * ty + side + 1, :] = rim[
                        across + side, at : at + 1, :
                    ]
                halo_out[1, way, 2 * ty + 2 : 2 * ty + 8, :] = jnp.zeros((6, nz), f32)
            correct(base, own_of(0, ty), beyond_of(0, ty))

        span = pl.ds(pl.multiple_of(c * small, small), small)

        def arrived(landed):
            pltpu.make_async_remote_copy(
                src_ref=landed,
                dst_ref=landed,
                send_sem=ex_send.at[0],
                recv_sem=ex_recv.at[c],
                device_id=to[0],
                device_id_type=MESH,
            ).wait_recv()

        pl.when(c == 0)(lambda: arrived(fields.at[:, slots:small]))
        pl.when(c > 0)(lambda: arrived(fields.at[:, span]))
        index = get(CELL, span)
        at = jnp.floor(index * (1.0 / nz))
        column_hot[:, span] = one_hot(at, columns)
        level_hot[:, span] = one_hot(index - nz * at, nz)
        press, start = sample(2, span)
        filtered = get(DRIVE, span) - get(FILT, span) * press
        gap = get(VESSEL, span) - start
        flux = get(PERM, span) * gap + filtered
        after = get(CARRIED, span) - get(BETA, span) * flux
        keep(GAP0, span, gap)
        keep(AFTER, span, after)
        keep(COUPLED, span, press)
        perm_here = get(PERM, span)
        edge = jnp.where(rim_column == at, 1.0, 0.0).astype(bf16)
        placed = lax.dot_general(
            jnp.concatenate(
                [column_hot[:, span] * column_of(half.astype(f32), columns) for half in halves(flux)]
                + [
                    edge * column_of(half.astype(f32), 4 * ty)
                    for value in (perm_here * after + filtered, perm_here)
                    for half in halves(value)
                ],
                axis=0,
            ),
            level_hot[:, span],
            (((1,), (1,)), ((), ())),
            preferred_element_type=f32,
        )
        total[0] += placed[0:columns] + placed[columns : 2 * columns]
        for i in range(2):
            first = 2 * columns + 8 * ty * i
            rim_total[i] += placed[first : first + 4 * ty] + placed[first + 4 * ty : first + 8 * ty]

    chunk = min(width, 2048)

    for x in range(tx):
        field[plane(x), :] = base[plane(x), :] + total[0, plane(x), :]
    stage(1, 0, lambda kind, x: field[plane(x), :])
    for c, (sx, sy) in enumerate(beside):
        at = sx * (tx - 1) * ty + sy * (ty - 1)
        corner_out[c] = field[at : at + 1, :]
    on_corners(lambda c: corner_copy(c, 3 - c).start())
    loads["observed"].wait()
    for x in range(tx):
        value = field[plane(x), :]
        second[plane(x), :] = (
            value
            + spread(lambda x: field[plane(x), :], x)
            - observed[x]
        )
    stage(1, ty, lambda kind, x: second[plane(x), :])
    for way in range(4):
        at = slice(way * ty, (way + 1) * ty)
        halo_out[1, way, ty : 2 * ty, :] += (
            rim_total[0, at, :] - rim_total[1, at, :] * halo_out[1, way, 0:ty, :]
        )
    send_halo(1)

    fill_table(0, field[...])

    @pl.loop(0, width // chunk)
    def _(c):
        span = pl.ds(pl.multiple_of(c * chunk, chunk), chunk)
        (middle,) = sample(1, span)
        perm_here = get(PERM, span)
        after = kept(AFTER, span)
        filtered = get(DRIVE, span) - get(FILT, span) * kept(COUPLED, span)
        keep(COUPLED, span, get(BETA, span) * perm_here)
        keep(GAP1, span, after - middle)
        deposit(1, [perm_here * after + filtered, perm_here], span)

    wait_halo(1)
    on_corners(lambda c: corner_copy(c, c).wait_recv())
    correct(second, own_of(1), beyond_of(1))
    for x in range(tx):
        second[plane(x), :] = mask[plane(x), :] * (
            second[plane(x), :]
            + (total[1, plane(x), :] - total[2, plane(x), :] * field[plane(x), :])
        )
    for way in range(4):
        outer = halo_in[1, way, 0:ty, :]
        value = halo_in[1, way, ty : 2 * ty, :] + rim[way] * (halo_out[1, way, 0:ty, :] - outer)
        for side in range(2):
            c = 2 * (way % 2) + side if way < 2 else 2 * side + way % 2
            edge = halo_in[1, way, 2 * ty + side : 2 * ty + side + 1, :] * (corner_in[c] - outer)
            value = value + jnp.where(inner_y == side * (ty - 1), edge, 0.0)
        ghost[way] = halo_in[0, way, 2 * ty : 3 * ty, :] * value
    stage(3, 0, lambda kind, x: second[plane(x), :])
    for x in range(tx):
        value = second[plane(x), :]
        field[plane(x), :] = (
            value + spread(lambda x: second[plane(x), :], x) - total[2, plane(x), :] * value
        )
    correct(field, own_of(3), lambda way: ghost[way])
    stage(2, 0, lambda kind, x: field[plane(x), :])
    send_halo(2)

    def give(k, d, where):
        return pltpu.make_async_remote_copy(
            src_ref=grad.at[:, lanes(k)],
            dst_ref=perm_back.at[me],
            send_sem=perm_send.at[0],
            recv_sem=perm_recv.at[0],
            device_id=where,
            device_id_type=MESH,
        )

    fill_table(0, second[...])
    fill_table(1, field[...])
    parts = width // chunk
    groups = n_gx // parts

    @pl.loop(0, parts)
    def _(i):
        span = pl.ds(pl.multiple_of((parts - 1 - i) * chunk, chunk), chunk)
        late, early = sample(2, span)
        grad[:, span] = (
            late * kept(GAP1, span) + (early - kept(COUPLED, span) * late) * kept(GAP0, span)
        )
        each_peer(i * groups, (i + 1) * groups, lambda k, d, where: give(k, d, where).start())

    perm_back[me] = grad[:, 0:slots]

    @pl.loop(0, parts)
    def _(c):
        span = pl.ds(pl.multiple_of(c * chunk, chunk), chunk)
        deposit(3, [kept(COUPLED, span) * get(PERM, span)], span)

    for x in range(tx):
        value = field[plane(x), :]
        base[plane(x), :] = (
            value
            + spread(lambda x: field[plane(x), :], x)
            - total[2, plane(x), :] * value
            + total[3, plane(x), :] * second[plane(x), :]
        )
    wait_halo(2)
    correct(base, own_of(2), beyond_of(2))
    for x in range(tx):
        out[x] = base[plane(x), :]

    sent_all = sent.at[0 : n - 1]
    pltpu.make_async_remote_copy(
        src_ref=sent_all,
        dst_ref=sent_all,
        send_sem=ex_send.at[0],
        recv_sem=ex_recv.at[0],
        device_id=to[0],
        device_id_type=MESH,
    ).wait_send()
    for phase in range(3):
        on_ways(lambda way: halo_copy(phase, way, way ^ 1).wait_send())
    on_corners(lambda c: corner_copy(c, 3 - c).wait_send())
    perm_all = perm_back.at[0 : n - 1]
    pltpu.make_async_remote_copy(
        src_ref=perm_all,
        dst_ref=perm_all,
        send_sem=perm_send.at[0],
        recv_sem=perm_recv.at[0],
        device_id=to[0],
        device_id_type=MESH,
    ).wait()
    for d in range(n):
        out_perm[0, d : d + 1, :] = perm_back[d] * active[d : d + 1, :]


def write_out(first, second, first_out, second_out, sem):
    copies = [
        pltpu.make_async_copy(first, first_out, sem.at[0]),
        pltpu.make_async_copy(second, second_out, sem.at[1]),
    ]
    for copy in copies:
        copy.start()
    for copy in copies:
        copy.wait()


def solution(mesh):
    n_gx, n_gy = mesh.shape["gx"], mesh.shape["gy"]
    n = n_gx * n_gy

    def shards(tracer, tensor, pressure, observed, depth, cell, *rest):
        tx, ty, nz = tracer.shape
        slots = cell.shape[2]
        width, columns = n * slots, tx * ty
        vmem = pl.BlockSpec(memory_space=pltpu.VMEM)
        tile = pltpu.VMEM((columns, nz), f32)
        block = pltpu.VMEM(cell.shape, f32)
        ints = pltpu.VMEM(cell.shape, jnp.int32)
        dma = pltpu.SemaphoreType.DMA
        results = pl.pallas_call(
            functools.partial(kernel, n_gx, n_gy),
            out_shape=(
                pltpu.VMEM(tracer.shape, f32),
                pltpu.VMEM(cell.shape, f32),
            ),
            in_specs=[pl.BlockSpec(memory_space=pl.ANY)] * 13,
            out_specs=(vmem, vmem),
            scratch_shapes=[
                pltpu.VMEM(tracer.shape, f32),
                pltpu.VMEM(tensor.shape, f32),
                pltpu.VMEM(tracer.shape, f32),
                pltpu.VMEM(tracer.shape, f32),
                pltpu.VMEM(depth.shape, jnp.int32),
                ints,
                ints,
                pltpu.VMEM((1, n), jnp.int32),
                block,
                block,
                block,
                block,
                block,
                pltpu.VMEM((n, slots), f32),
                pltpu.VMEM((n, 8, slots), f32),
                pltpu.VMEM((8, width), f32),
                pltpu.VMEM((slots, width), bf16),
                pltpu.VMEM((1, width), f32),
                pltpu.VMEM((1, width), f32),
                pltpu.VMEM((nz, width), bf16),
                pltpu.VMEM((columns, width), bf16),
                pltpu.VMEM((8, width), f32),
                pltpu.VMEM((1, width), f32),
                pltpu.VMEM((2 * columns, 2 * nz), bf16),
                tile,
                tile,
                tile,
                pltpu.VMEM((4, columns, nz), f32),
                tile,
                tile,
                tile,
                tile,
                pltpu.VMEM((4, ty, nz), f32),
                pltpu.VMEM((2, 4 * ty, nz), f32),
                pltpu.VMEM((4, ty, nz), f32),
                pltpu.VMEM((4, 4, 3 * ty, nz), f32),
                pltpu.VMEM((3, 4, 3 * ty, nz), f32),
                pltpu.VMEM((4, 1, nz), f32),
                pltpu.VMEM((4, 1, nz), f32),
                pltpu.VMEM((n, 1, slots), f32),
                dma((1,)),
                dma((n // 8,)),
                dma((3, 4)),
                dma((3, 4)),
                dma((4,)),
                dma((4,)),
                dma((1,)),
                dma((1,)),
                dma((13,)),
            ],
            compiler_params=pltpu.CompilerParams(
                collective_id=0, has_side_effects=True, vmem_limit_bytes=56 << 20
            ),
        )(tracer, tensor, pressure, observed, depth, cell, *rest)
        results = [pltpu.with_memory_space_constraint(r, pltpu.VMEM) for r in results]
        anywhere = pl.BlockSpec(memory_space=pl.ANY)
        return pl.pallas_call(
            write_out,
            out_shape=tuple(jax.ShapeDtypeStruct(r.shape, f32) for r in results),
            in_specs=[anywhere, anywhere],
            out_specs=(anywhere, anywhere),
            scratch_shapes=[dma((2,))],
        )(*results)

    return jax.shard_map(
        shards,
        mesh=mesh,
        in_specs=(
            P("gx", "gy", None),
            P(None, "gx", "gy", None),
            P("gx", "gy", None),
            P("gx", "gy", None),
            P("gx", "gy"),
            P(("gx", "gy"), None, None),
            P(("gx", "gy"), None, None),
            P(("gx", "gy"), None),
            P(("gx", "gy"), None, None),
            P(("gx", "gy"), None, None),
            P(("gx", "gy"), None, None),
            P(("gx", "gy"), None, None),
            P(("gx", "gy"), None, None),
        ),
        out_specs=(P("gx", "gy", None), P(("gx", "gy"), None, None)),
        check_vma=False,
    )
```

```python
import functools

import jax
import jax.numpy as jnp
from jax import lax
from jax.experimental import pallas as pl
from jax.experimental.pallas import tpu as pltpu
from jax.sharding import PartitionSpec as P

MESH = pl.DeviceIdType.MESH
upwind_rate = 0.3
f32, bf16 = jnp.float32, jnp.bfloat16
CELL, VESSEL, CARRIED, PERM, FILT, DRIVE, BETA = range(7)
GAP0, AFTER, GAP1, COUPLED = range(4)


def harmonic(lower_k, upper_k):
    return 2.0 * lower_k * upper_k / (lower_k + upper_k)


def halves(x):
    high = x.astype(bf16)
    return high, (x - high.astype(f32)).astype(bf16)


def column_of(row, count):
    tile = jnp.broadcast_to(row, (16, row.shape[1])).astype(bf16)
    return jnp.concatenate([tile] * (count // 16), axis=0)


def one_hot(row, count):
    position = lax.broadcasted_iota(jnp.int32, (count, row.shape[1]), 0).astype(f32)
    return jnp.where(position == row, 1.0, 0.0).astype(bf16)


def kernel(n_gx, n_gy, *refs):
    (
        tracer_in,
        tensor_in,
        pressure_in,
        observed_in,
        depth_in,
        cell_in,
        parent_in,
        counts_in,
        perm_in_hbm,
        filt_in,
        seg_pressure_in,
        seg_tracer_in,
        beta_in,
        out,
        out_perm,
        tracer,
        tensor,
        pressure,
        observed,
        depth,
        cell,
        parent,
        counts,
        perm,
        filt,
        drive,
        seg_tracer,
        beta,
        active,
        sent,
        fields,
        parent_hot,
        parent_group,
        carried,
        level_hot,
        column_hot,
        rows,
        grad,
        table,
        field,
        second,
        base,
        total,
        face_x,
        face_y,
        face_z,
        mask,
        rim,
        rim_total,
        ghost,
        halo_out,
        halo_in,
        corner_out,
        corner_in,
        perm_back,
        ex_send,
        ex_recv,
        halo_send,
        halo_recv,
        corner_send,
        corner_recv,
        perm_send,
        perm_recv,
        load_sem,
    ) = refs
    n = n_gx * n_gy
    loads = {}
    for i, (name, source, held) in enumerate(
        (
            ("parent", parent_in, parent),
            ("vessel", seg_tracer_in, seg_tracer),
            ("counts", counts_in, counts),
            ("cell", cell_in, cell),
            ("perm", perm_in_hbm, perm),
            ("filt", filt_in, filt),
            ("drive", seg_pressure_in, drive),
            ("beta", beta_in, beta),
            ("depth", depth_in, depth),
            ("tracer", tracer_in, tracer),
            ("tensor", tensor_in, tensor),
            ("pressure", pressure_in, pressure),
            ("observed", observed_in, observed),
        )
    ):
        loads[name] = pltpu.make_async_copy(source, held, load_sem.at[i])
        loads[name].start()
    gx, gy = lax.axis_index("gx"), lax.axis_index("gy")
    me = gx * n_gy + gy
    tx, ty, nz = tracer.shape
    columns = tx * ty
    slots = cell.shape[2]
    width = n * slots

    barrier = pltpu.get_barrier_semaphore()

    def turns(value, count):
        bits = []
        for b in range(count.bit_length() - 1):
            bits.append((2**b, (1 - 2 * lax.rem(lax.div(value, 2**b), 2)) * 2**b))
        return bits

    turns_x, turns_y = turns(gx, n_gx), turns(gy, n_gy)

    def peer_x(j):
        x = gx
        for size, turn in turns_x:
            x = x + lax.rem(lax.div(j, size), 2) * turn
        return x

    peers_y = []
    for l in range(n_gy):
        y = gy
        for size, turn in turns_y:
            if l // size % 2:
                y = y + turn
        peers_y.append(y)

    def each_peer(first, last, body):
        @pl.loop(first, last)
        def _(i):
            j = n_gx - 1 - i
            x = peer_x(j)
            for l in reversed(range(n_gy)):
                y = peers_y[l]
                if l:
                    body(j * n_gy + l, x * n_gy + y, (x, y))
                else:

                    @pl.when(j > 0)
                    def _(y=y):
                        body(j * n_gy, x * n_gy + y, (x, y))

    each_peer(
        0,
        n_gx,
        lambda k, d, where: pl.semaphore_signal(
            barrier, inc=1, device_id=where, device_id_type=MESH
        ),
    )

    loads["parent"].wait()
    for g in range(n // 8):
        block = parent[0, 8 * g : 8 * g + 8, :]
        lane = (block & (slots - 1)).astype(f32)
        group = (block // slots).astype(f32)
        for r in range(8):
            at = (8 * g + r) * slots
            parent_hot[:, at : at + slots] = one_hot(lane[r : r + 1, :], slots)
            parent_group[:, at : at + slots] = group[r : r + 1, :]
    loads["vessel"].wait()
    high, low = halves(seg_tracer[0])
    step = 1024

    @pl.loop(0, width // step)
    def _(c):
        span = pl.ds(pl.multiple_of(c * step, step), step)
        picked = jnp.dot(high, parent_hot[:, span], preferred_element_type=f32) + jnp.dot(
            low, parent_hot[:, span], preferred_element_type=f32
        )
        position = lax.broadcasted_iota(jnp.int32, (n, step), 0).astype(f32)
        upstream = jnp.sum(
            jnp.where(position == parent_group[:, span], picked, 0.0), axis=0, keepdims=True
        )
        carried[:, span] = upwind_rate * upstream

    for name in ("counts", "cell", "perm", "filt", "drive", "beta"):
        loads[name].wait()
    diagonal = lax.broadcasted_iota(jnp.int32, (n, n), 0) == lax.broadcasted_iota(
        jnp.int32, (n, n), 1
    )
    live = jnp.broadcast_to(counts[...].astype(f32), (n, n))
    live = jnp.sum(jnp.where(diagonal, live, 0.0), axis=1, keepdims=True)
    slot = lax.broadcasted_iota(jnp.int32, (n, slots), 1).astype(f32)
    active[...] = jnp.where(slot < live, 1.0, 0.0)
    perm[0] = perm[0] * active[...]
    filt[0] = filt[0] * active[...]
    drive[0] = drive[0] * filt[0]
    for d in range(n):
        at = slice(d * slots, (d + 1) * slots)
        vessel = seg_tracer[0, d : d + 1, :]
        sent[d, CELL : CELL + 1, :] = cell[0, d : d + 1, :].astype(f32)
        sent[d, VESSEL : VESSEL + 1, :] = vessel
        sent[d, CARRIED : CARRIED + 1, :] = (1.0 - upwind_rate) * vessel + carried[:, at]
        sent[d, PERM : PERM + 1, :] = perm[0, d : d + 1, :]
        sent[d, FILT : FILT + 1, :] = filt[0, d : d + 1, :]
        sent[d, DRIVE : DRIVE + 1, :] = drive[0, d : d + 1, :]
        sent[d, BETA : BETA + 1, :] = beta[0, d : d + 1, :]
        sent[d, BETA + 1 : BETA + 2, :] = jnp.zeros((1, slots), f32)

    has = (gx > 0, gx < n_gx - 1, gy > 0, gy < n_gy - 1)
    to = ((gx - 1, gy), (gx + 1, gy), (gx, gy - 1), (gx, gy + 1))
    held_rows = (3 * ty, 2 * ty + 8, ty)

    def plane(x):
        return slice(x * ty, (x + 1) * ty)

    def halo_copy(phase, way, landing):
        held = pl.ds(0, held_rows[phase])
        return pltpu.make_async_remote_copy(
            src_ref=halo_out.at[phase, way, held],
            dst_ref=halo_in.at[phase, landing, held],
            send_sem=halo_send.at[phase, way],
            recv_sem=halo_recv.at[phase, landing],
            device_id=to[way],
            device_id_type=MESH,
        )

    def on_ways(body):
        for way in range(4):

            @pl.when(has[way])
            def _(way=way):
                body(way)

    def send_halo(phase):
        on_ways(lambda way: halo_copy(phase, way, way ^ 1).start())

    def wait_halo(phase):
        on_ways(lambda way: halo_copy(phase, way, way).wait_recv())

    beside = [(sx, sy) for sx in (0, 1) for sy in (0, 1)]

    def corner_copy(c, landing):
        sx, sy = beside[c]
        return pltpu.make_async_remote_copy(
            src_ref=corner_out.at[c],
            dst_ref=corner_in.at[landing],
            send_sem=corner_send.at[c],
            recv_sem=corner_recv.at[landing],
            device_id=(gx + 2 * sx - 1, gy + 2 * sy - 1),
            device_id_type=MESH,
        )

    def on_corners(body):
        for c, (sx, sy) in enumerate(beside):

            @pl.when(jnp.logical_and(has[sx], has[2 + sy]))
            def _(c=c):
                body(c)

    def stage(phase, first, source):
        halo_out[phase, 0, first : first + ty, :] = source(0, 0)
        halo_out[phase, 1, first : first + ty, :] = source(0, tx - 1)
        for x in range(tx):
            held = source(1, x)
            halo_out[phase, 2, first + x : first + x + 1, :] = held[0:1, :]
            halo_out[phase, 3, first + x : first + x + 1, :] = held[ty - 1 : ty, :]

    inner_y = lax.broadcasted_iota(jnp.int32, (ty, nz), 0)
    inner_z = lax.broadcasted_iota(jnp.int32, (ty, nz), 1)
    square = lax.broadcasted_iota(jnp.int32, (ty, ty), 0) == lax.broadcasted_iota(
        jnp.int32, (ty, ty), 1
    )
    for way in range(4):

        @pl.when(jnp.logical_not(has[way]))
        def _(way=way):
            for phase in range(3):
                halo_in[phase, way] = jnp.zeros((3 * ty, nz), f32)

    for c, (sx, sy) in enumerate(beside):

        @pl.when(jnp.logical_not(jnp.logical_and(has[sx], has[2 + sy])))
        def _(c=c):
            corner_in[c] = jnp.zeros((1, nz), f32)

    def lanes(k):
        return pl.ds(pl.multiple_of(k * slots, slots), slots)

    together = 8
    small = together * slots

    def exchange(k, d, where):
        return pltpu.make_async_remote_copy(
            src_ref=sent.at[d],
            dst_ref=fields.at[:, lanes(k)],
            send_sem=ex_send.at[0],
            recv_sem=ex_recv.at[lax.div(k, together)],
            device_id=where,
            device_id_type=MESH,
        )

    pl.semaphore_wait(barrier, n - 1)
    each_peer(0, n_gx, lambda k, d, where: exchange(k, d, where).start())
    fields[:, 0:slots] = sent[me]
    loads["depth"].wait()
    for x in range(tx):
        deep = jnp.broadcast_to(depth[x : x + 1, :].astype(f32), (ty, ty))
        deep = jnp.sum(jnp.where(square, deep, 0.0), axis=1, keepdims=True)
        mask[plane(x), :] = jnp.where(inner_z.astype(f32) < deep, 1.0, 0.0)
    loads["tracer"].wait()
    loads["tensor"].wait()
    stage(0, 0, lambda kind, x: tensor[kind, x])
    stage(0, ty, lambda kind, x: tracer[x])
    stage(0, 2 * ty, lambda kind, x: mask[plane(x), :])
    send_halo(0)

    for x in range(tx):
        k = tensor[2, x]
        face_z[plane(x), :] = jnp.where(inner_z == nz - 1, 0.0, harmonic(k, pltpu.roll(k, nz - 1, 1)))
        k = tensor[1, x]
        face_y[plane(x), :] = jnp.where(inner_y == ty - 1, 0.0, harmonic(k, pltpu.roll(k, ty - 1, 0)))
        if x:
            face_x[plane(x), :] = harmonic(tensor[0, x - 1], tensor[0, x])

    def spread(read, x):
        value = read(x)
        flow = face_y[plane(x), :] * (pltpu.roll(value, ty - 1, 0) - value)
        result = flow - pltpu.roll(flow, 1, 0)
        flow = face_z[plane(x), :] * (pltpu.roll(value, nz - 1, 1) - value)
        result = result + (flow - pltpu.roll(flow, 1, 1))
        if x:
            result = result - face_x[plane(x), :] * (value - read(x - 1))
        if x < tx - 1:
            result = result + face_x[plane(x + 1), :] * (read(x + 1) - value)
        return result

    def correct(target, own, beyond):
        for way in range(2):
            at = plane(way * (tx - 1))
            target[at, :] += rim[way] * (beyond(way) - own(way))
        for way in range(2, 4):
            extra = rim[way] * (beyond(way) - own(way))
            for x in range(tx):
                at = x * ty + (way - 2) * (ty - 1)
                target[at : at + 1, :] += extra[x : x + 1, :]

    def own_of(phase, first=0):
        return lambda way: halo_out[phase, way, first : first + ty, :]

    def beyond_of(phase, first=0):
        return lambda way: halo_in[phase, way, first : first + ty, :]

    for x in range(tx):
        base[plane(x), :] = tracer[x] + spread(lambda x: tracer[x], x)

    def fill_table(first, read):
        high, low = halves(read)
        table[first * columns : (first + 1) * columns, 0:nz] = high
        table[first * columns : (first + 1) * columns, nz : 2 * nz] = low

    loads["pressure"].wait()
    fill_table(0, pressure[...].reshape(columns, nz))
    fill_table(1, tracer[...].reshape(columns, nz))

    def sample(count, span):
        hot = level_hot[:, span]
        picked = jnp.dot(
            table[0 : count * columns, :],
            jnp.concatenate([hot, hot], axis=0),
            preferred_element_type=f32,
        )
        chosen = column_hot[:, span].astype(f32)
        return [
            jnp.sum(picked[i * columns : (i + 1) * columns] * chosen, axis=0, keepdims=True)
            for i in range(count)
        ]

    def deposit(first, values, span):
        hot = column_hot[:, span]
        contract = (((1,), (1,)), ((), ()))
        placed = lax.dot_general(
            jnp.concatenate(
                [
                    hot * column_of(half.astype(f32), columns)
                    for value in values
                    for half in halves(value)
                ],
                axis=0,
            ),
            level_hot[:, span],
            contract,
            preferred_element_type=f32,
        )
        for i in range(len(values)):
            at = 2 * i * columns
            total[first + i] += placed[at : at + columns] + placed[at + columns : at + 2 * columns]

    def get(name, span):
        return fields[name : name + 1, span]

    def keep(name, span, value):
        rows[name : name + 1, span] = value

    def kept(name, span):
        return rows[name : name + 1, span]

    total[...] = jnp.zeros_like(total)
    rim_total[...] = jnp.zeros_like(rim_total)
    place = lax.broadcasted_iota(jnp.int32, (4 * ty, small), 0).astype(f32)
    rim_column = jnp.where(
        place < 2 * ty,
        jnp.where(place < ty, place, place + (columns - 2 * ty)),
        jnp.where(place < 3 * ty, (place - 2 * ty) * ty, (place - 3 * ty) * ty + (ty - 1)),
    )
    @pl.loop(0, n // together)
    def _(c):
        @pl.when(c == n // together - 1)
        def _():
            wait_halo(0)
            for way in range(4):
                rim[way] = harmonic(halo_in[0, way, 0:ty, :], halo_out[0, way, 0:ty, :])
            for way in range(4):
                across = 2 - way // 2 * 2
                at = way % 2 * (ty - 1)
                for side in range(2):
                    halo_out[1, way, 2 * ty + side : 2 * ty + side + 1, :] = rim[
                        across + side, at : at + 1, :
                    ]
                halo_out[1, way, 2 * ty + 2 : 2 * ty + 8, :] = jnp.zeros((6, nz), f32)
            correct(base, own_of(0, ty), beyond_of(0, ty))

        span = pl.ds(pl.multiple_of(c * small, small), small)

        def arrived(landed):
            pltpu.make_async_remote_copy(
                src_ref=landed,
                dst_ref=landed,
                send_sem=ex_send.at[0],
                recv_sem=ex_recv.at[c],
                device_id=to[0],
                device_id_type=MESH,
            ).wait_recv()

        pl.when(c == 0)(lambda: arrived(fields.at[:, slots:small]))
        pl.when(c > 0)(lambda: arrived(fields.at[:, span]))
        index = get(CELL, span)
        at = jnp.floor(index * (1.0 / nz))
        column_hot[:, span] = one_hot(at, columns)
        level_hot[:, span] = one_hot(index - nz * at, nz)
        press, start = sample(2, span)
        filtered = get(DRIVE, span) - get(FILT, span) * press
        gap = get(VESSEL, span) - start
        flux = get(PERM, span) * gap + filtered
        after = get(CARRIED, span) - get(BETA, span) * flux
        keep(GAP0, span, gap)
        keep(AFTER, span, after)
        keep(COUPLED, span, press)
        perm_here = get(PERM, span)
        edge = jnp.where(rim_column == at, 1.0, 0.0).astype(bf16)
        placed = lax.dot_general(
            jnp.concatenate(
                [column_hot[:, span] * column_of(half.astype(f32), columns) for half in halves(flux)]
                + [
                    edge * column_of(half.astype(f32), 4 * ty)
                    for value in (perm_here * after + filtered, perm_here)
                    for half in halves(value)
                ],
                axis=0,
            ),
            level_hot[:, span],
            (((1,), (1,)), ((), ())),
            preferred_element_type=f32,
        )
        total[0] += placed[0:columns] + placed[columns : 2 * columns]
        for i in range(2):
            first = 2 * columns + 8 * ty * i
            rim_total[i] += placed[first : first + 4 * ty] + placed[first + 4 * ty : first + 8 * ty]

    chunk = min(width, 2048)

    for x in range(tx):
        field[plane(x), :] = base[plane(x), :] + total[0, plane(x), :]
    stage(1, 0, lambda kind, x: field[plane(x), :])
    for c, (sx, sy) in enumerate(beside):
        at = sx * (tx - 1) * ty + sy * (ty - 1)
        corner_out[c] = field[at : at + 1, :]
    on_corners(lambda c: corner_copy(c, 3 - c).start())
    loads["observed"].wait()
    for x in range(tx):
        value = field[plane(x), :]
        second[plane(x), :] = (
            value
            + spread(lambda x: field[plane(x), :], x)
            - observed[x]
        )
    stage(1, ty, lambda kind, x: second[plane(x), :])
    for way in range(4):
        at = slice(way * ty, (way + 1) * ty)
        halo_out[1, way, ty : 2 * ty, :] += (
            rim_total[0, at, :] - rim_total[1, at, :] * halo_out[1, way, 0:ty, :]
        )
    send_halo(1)

    fill_table(0, field[...])

    @pl.loop(0, width // chunk)
    def _(c):
        span = pl.ds(pl.multiple_of(c * chunk, chunk), chunk)
        (middle,) = sample(1, span)
        perm_here = get(PERM, span)
        after = kept(AFTER, span)
        filtered = get(DRIVE, span) - get(FILT, span) * kept(COUPLED, span)
        keep(COUPLED, span, get(BETA, span) * perm_here)
        keep(GAP1, span, after - middle)
        deposit(1, [perm_here * after + filtered, perm_here], span)

    wait_halo(1)
    on_corners(lambda c: corner_copy(c, c).wait_recv())
    correct(second, own_of(1), beyond_of(1))
    for x in range(tx):
        second[plane(x), :] = mask[plane(x), :] * (
            second[plane(x), :]
            + (total[1, plane(x), :] - total[2, plane(x), :] * field[plane(x), :])
        )
    for way in range(4):
        outer = halo_in[1, way, 0:ty, :]
        value = halo_in[1, way, ty : 2 * ty, :] + rim[way] * (halo_out[1, way, 0:ty, :] - outer)
        for side in range(2):
            c = 2 * (way % 2) + side if way < 2 else 2 * side + way % 2
            edge = halo_in[1, way, 2 * ty + side : 2 * ty + side + 1, :] * (corner_in[c] - outer)
            value = value + jnp.where(inner_y == side * (ty - 1), edge, 0.0)
        ghost[way] = halo_in[0, way, 2 * ty : 3 * ty, :] * value
    stage(3, 0, lambda kind, x: second[plane(x), :])
    for x in range(tx):
        value = second[plane(x), :]
        field[plane(x), :] = (
            value + spread(lambda x: second[plane(x), :], x) - total[2, plane(x), :] * value
        )
    correct(field, own_of(3), lambda way: ghost[way])
    stage(2, 0, lambda kind, x: field[plane(x), :])
    send_halo(2)

    def give(k, d, where):
        return pltpu.make_async_remote_copy(
            src_ref=grad.at[:, lanes(k)],
            dst_ref=perm_back.at[me],
            send_sem=perm_send.at[0],
            recv_sem=perm_recv.at[0],
            device_id=where,
            device_id_type=MESH,
        )

    fill_table(0, second[...])
    fill_table(1, field[...])
    chunk = min(width, 4096)
    parts = width // chunk
    groups = n_gx // parts

    @pl.loop(0, parts)
    def _(i):
        span = pl.ds(pl.multiple_of((parts - 1 - i) * chunk, chunk), chunk)
        late, early = sample(2, span)
        grad[:, span] = (
            late * kept(GAP1, span) + (early - kept(COUPLED, span) * late) * kept(GAP0, span)
        )
        each_peer(i * groups, (i + 1) * groups, lambda k, d, where: give(k, d, where).start())

    perm_back[me] = grad[:, 0:slots]

    fine = 512

    @pl.loop(0, width // fine)
    def _(c):
        span = pl.ds(pl.multiple_of(c * fine, fine), fine)
        deposit(3, [kept(COUPLED, span) * get(PERM, span)], span)

    for x in range(tx):
        value = field[plane(x), :]
        base[plane(x), :] = (
            value
            + spread(lambda x: field[plane(x), :], x)
            - total[2, plane(x), :] * value
            + total[3, plane(x), :] * second[plane(x), :]
        )
    wait_halo(2)
    correct(base, own_of(2), beyond_of(2))
    for x in range(tx):
        out[x] = base[plane(x), :]

    sent_all = sent.at[0 : n - 1]
    pltpu.make_async_remote_copy(
        src_ref=sent_all,
        dst_ref=sent_all,
        send_sem=ex_send.at[0],
        recv_sem=ex_recv.at[0],
        device_id=to[0],
        device_id_type=MESH,
    ).wait_send()
    for phase in range(3):
        on_ways(lambda way: halo_copy(phase, way, way ^ 1).wait_send())
    on_corners(lambda c: corner_copy(c, 3 - c).wait_send())
    perm_all = perm_back.at[0 : n - 1]
    pltpu.make_async_remote_copy(
        src_ref=perm_all,
        dst_ref=perm_all,
        send_sem=perm_send.at[0],
        recv_sem=perm_recv.at[0],
        device_id=to[0],
        device_id_type=MESH,
    ).wait()
    for d in range(n):
        out_perm[0, d : d + 1, :] = perm_back[d] * active[d : d + 1, :]


def write_out(first, second, first_out, second_out, sem):
    copies = [
        pltpu.make_async_copy(first, first_out, sem.at[0]),
        pltpu.make_async_copy(second, second_out, sem.at[1]),
    ]
    for copy in copies:
        copy.start()
    for copy in copies:
        copy.wait()


def solution(mesh):
    n_gx, n_gy = mesh.shape["gx"], mesh.shape["gy"]
    n = n_gx * n_gy

    def shards(tracer, tensor, pressure, observed, depth, cell, *rest):
        tx, ty, nz = tracer.shape
        slots = cell.shape[2]
        width, columns = n * slots, tx * ty
        vmem = pl.BlockSpec(memory_space=pltpu.VMEM)
        tile = pltpu.VMEM((columns, nz), f32)
        block = pltpu.VMEM(cell.shape, f32)
        ints = pltpu.VMEM(cell.shape, jnp.int32)
        dma = pltpu.SemaphoreType.DMA
        results = pl.pallas_call(
            functools.partial(kernel, n_gx, n_gy),
            out_shape=(
                pltpu.VMEM(tracer.shape, f32),
                pltpu.VMEM(cell.shape, f32),
            ),
            in_specs=[pl.BlockSpec(memory_space=pl.ANY)] * 13,
            out_specs=(vmem, vmem),
            scratch_shapes=[
                pltpu.VMEM(tracer.shape, f32),
                pltpu.VMEM(tensor.shape, f32),
                pltpu.VMEM(tracer.shape, f32),
                pltpu.VMEM(tracer.shape, f32),
                pltpu.VMEM(depth.shape, jnp.int32),
                ints,
                ints,
                pltpu.VMEM((1, n), jnp.int32),
                block,
                block,
                block,
                block,
                block,
                pltpu.VMEM((n, slots), f32),
                pltpu.VMEM((n, 8, slots), f32),
                pltpu.VMEM((8, width), f32),
                pltpu.VMEM((slots, width), bf16),
                pltpu.VMEM((1, width), f32),
                pltpu.VMEM((1, width), f32),
                pltpu.VMEM((nz, width), bf16),
                pltpu.VMEM((columns, width), bf16),
                pltpu.VMEM((8, width), f32),
                pltpu.VMEM((1, width), f32),
                pltpu.VMEM((2 * columns, 2 * nz), bf16),
                tile,
                tile,
                tile,
                pltpu.VMEM((4, columns, nz), f32),
                tile,
                tile,
                tile,
                tile,
                pltpu.VMEM((4, ty, nz), f32),
                pltpu.VMEM((2, 4 * ty, nz), f32),
                pltpu.VMEM((4, ty, nz), f32),
                pltpu.VMEM((4, 4, 3 * ty, nz), f32),
                pltpu.VMEM((3, 4, 3 * ty, nz), f32),
                pltpu.VMEM((4, 1, nz), f32),
                pltpu.VMEM((4, 1, nz), f32),
                pltpu.VMEM((n, 1, slots), f32),
                dma((1,)),
                dma((n // 8,)),
                dma((3, 4)),
                dma((3, 4)),
                dma((4,)),
                dma((4,)),
                dma((1,)),
                dma((1,)),
                dma((13,)),
            ],
            compiler_params=pltpu.CompilerParams(
                collective_id=0, has_side_effects=True, vmem_limit_bytes=56 << 20
            ),
        )(tracer, tensor, pressure, observed, depth, cell, *rest)
        results = [pltpu.with_memory_space_constraint(r, pltpu.VMEM) for r in results]
        anywhere = pl.BlockSpec(memory_space=pl.ANY)
        return pl.pallas_call(
            write_out,
            out_shape=tuple(jax.ShapeDtypeStruct(r.shape, f32) for r in results),
            in_specs=[anywhere, anywhere],
            out_specs=(anywhere, anywhere),
            scratch_shapes=[dma((2,))],
        )(*results)

    return jax.shard_map(
        shards,
        mesh=mesh,
        in_specs=(
            P("gx", "gy", None),
            P(None, "gx", "gy", None),
            P("gx", "gy", None),
            P("gx", "gy", None),
            P("gx", "gy"),
            P(("gx", "gy"), None, None),
            P(("gx", "gy"), None, None),
            P(("gx", "gy"), None),
            P(("gx", "gy"), None, None),
            P(("gx", "gy"), None, None),
            P(("gx", "gy"), None, None),
            P(("gx", "gy"), None, None),
            P(("gx", "gy"), None, None),
        ),
        out_specs=(P("gx", "gy", None), P(("gx", "gy"), None, None)),
        check_vma=False,
    )
```
